32 devices in a mesh: win: 4 (over y, x), seq: 8 (over z, core).
Axes of the slice: x: 2, y: 2, z: 4, core: 2. Of those that a mesh axis runs over, the one named last changes fastest.
Arguments:
- tokens: bfloat16 [8, 1024, 768], P('win', 'seq'), may hold values from -6 to 6
- cotangent: bfloat16 [8, 1024, 768], P('win', 'seq'), may hold values from -6 to 6
- group_ids: int32 [8], P('win'), may hold values from 0 to 7
- random_blocks: int32 [8, 16, 3], P('win'), may hold values from 0 to 15, as said below
- norm1_gain: float32 [768], replicated, may hold values from 0.25 to 1.75
- norm1_bias: float32 [768], replicated, may hold values from -1.25 to 1.25
- query_weight: bfloat16 [768, 768], replicated, may hold values from -0.21875 to 0.21875
- query_bias: float32 [768], replicated, may hold values from -1.25 to 1.25
- key_weight: bfloat16 [768, 768], replicated, may hold values from -0.21875 to 0.21875
- value_weight: bfloat16 [768, 768], replicated, may hold values from -0.21875 to 0.21875
- value_bias: float32 [768], replicated, may hold values from -1.25 to 1.25
- out_weight: bfloat16 [768, 768], replicated, may hold values from -1.75 to 1.75
- out_bias: float32 [768], replicated, may hold values from -1.25 to 1.25
- norm2_gain: float32 [768], replicated, may hold values from 0.25 to 1.75
- norm2_bias: float32 [768], replicated, may hold values from -1.25 to 1.25
- up_weight: bfloat16 [768, 3072], replicated, may hold values from -0.21875 to 0.21875
- up_bias: float32 [3072], replicated, may hold values from -1.25 to 1.25
- down_weight: bfloat16 [3072, 768], replicated, may hold values from -0.109375 to 0.109375
- down_bias: float32 [768], replicated, may hold values from -1.25 to 1.25
Outputs:
- output: bfloat16 [8, 1024, 768], P('win', 'seq')
- input_grad: bfloat16 [8, 1024, 768], P('win', 'seq')
- norm1_gain_grad: float32 [768], replicated
- norm1_bias_grad: float32 [768], replicated
- query_weight_grad: float32 [768, 768], replicated
- query_bias_grad: float32 [768], replicated
- key_weight_grad: float32 [768, 768], replicated
- value_weight_grad: float32 [768, 768], replicated
- value_bias_grad: float32 [768], replicated
- out_weight_grad: float32 [768, 768], replicated
- out_bias_grad: float32 [768], replicated
- norm2_gain_grad: float32 [768], replicated
- norm2_bias_grad: float32 [768], replicated
- up_weight_grad: float32 [768, 3072], replicated
- up_bias_grad: float32 [3072], replicated
- down_weight_grad: float32 [3072, 768], replicated
- down_bias_grad: float32 [768], replicated
The draws below stay inside these ranges and needn't reach their ends.
Inputs may be any that keep to these rules, and one draw needn't show every extreme that they name: `random_blocks`: take the windows in aligned groups of 1 (one micro-batch of one index of win) and the blocks in aligned runs of 2 (block b lies in run b // 2). Within one group of windows, the 6 random entries of the query blocks of one run name blocks of any one run at most 1 times, and in every group some run names blocks of one run exactly 1 times.
All inputs are finite; a program needn't handle non-finite values.
Results may differ from the reference program's by a relative error of at most 0.014.
Values may be sent and summed in bfloat16 or wider, within the bound.
A program may use at most 256 MiB of HBM per device.

```python
import math
import jax
import jax.numpy as jnp
import numpy as np
from jax import lax

D = 768
HEADS = 12
HEAD_DIM = 64
FF = 3072
BLOCK = 64
RAND = 3
BLK_DEV = 2
WIN_MB = 1
GROUPS = 8
NB = 16
LENGTH = 1024
WINDOWS = 8
CAP = 1


def draw_random_blocks(key, part):
    owner_count = NB // BLK_DEV
    slot_count = owner_count * CAP
    wanted = WIN_MB * BLK_DEV * RAND
    group_count = WINDOWS // WIN_MB * owner_count
    group_keys = jax.random.split(jax.random.fold_in(key, 7), group_count)

    def one_group(group_key):
        key_order, key_full, key_shuffle, key_within = jax.random.split(group_key, 4)
        priority = jax.random.permutation(key_order, slot_count)
        full_owner = jax.random.randint(key_full, (), 0, owner_count)
        holder = jnp.arange(slot_count) // CAP
        scores = jnp.where(holder == full_owner, priority - slot_count, priority)
        taken_slots = jnp.argsort(scores)[:wanted]
        chosen = jax.random.permutation(key_shuffle, taken_slots // CAP)
        within = jax.random.randint(key_within, (wanted,), 0, BLK_DEV)
        return (chosen * BLK_DEV + within).astype(jnp.int32)
    values = jax.vmap(one_group)(group_keys)
    values = values.reshape(WINDOWS // WIN_MB, owner_count, WIN_MB, BLK_DEV, RAND)
    values = jnp.transpose(values, (0, 2, 1, 3, 4))
    return values.reshape(WINDOWS, NB, RAND)


def touch_ends(drawn, key, low, top_value):
    longest = drawn.shape.index(max(drawn.shape))
    spots = []
    for shift in (0, 1):
        where = [jax.random.randint(jax.random.fold_in(key, axis), (), 0, length) for axis, length in enumerate(drawn.shape)]
        where[longest] = (where[longest] + shift) % drawn.shape[longest]
        spots.append(tuple(where))
    return drawn.at[spots[0]].set(low).at[spots[1]].set(top_value)


def levels(own_key, extent, cuts, smallest, high):
    loudness = 1.0
    for axis_at, shards_of in cuts:
        heights = jax.random.uniform(jax.random.fold_in(jax.random.fold_in(own_key, 6), axis_at), (shards_of,), jnp.float32, smallest / len(cuts), high / len(cuts))
        loudness = loudness * jnp.repeat(jnp.exp(heights), extent[axis_at] // shards_of).reshape((-1,) + (1,) * (len(extent) - 1 - axis_at))
    return loudness


def cumulative_ranks(count, lean):
    weights = [(1 << 20) // math.isqrt(standing ** lean) + 1 for standing in range(1, count + 1)]
    scale = 1 + sum(weights) // (1 << 30)
    return np.cumsum(np.array([max(1, weight // scale) for weight in weights]))


def ranked(stream_key, shape, count, lean):
    grid = cumulative_ranks(count, lean)
    ticket = jax.random.randint(jax.random.fold_in(stream_key, 1), shape, 0, int(grid[count - 1]))
    grade = jnp.searchsorted(jnp.asarray(grid, jnp.int32), ticket, side="right")
    return jax.random.permutation(jax.random.fold_in(stream_key, 2), count)[grade].astype(jnp.int32)


def scatter_about(key, dims, width, reach, cuts=(), held_as=jnp.bfloat16):
    drawn = jax.random.normal(key, dims, jnp.float32) * width
    if len(cuts) > 0:
        drawn = levels(key, dims, cuts, -0.22, 0.18) * drawn
    return jnp.clip(drawn, min=-reach, max=reach).astype(held_as)


def setup_inputs(seed: int = 0) -> dict:
    arg_keys = jax.random.split(jax.random.key(seed), 20)
    return {
        "tokens": scatter_about(arg_keys[0], (WINDOWS, LENGTH, D), 1.0, 6.0, ((0, 4), (1, 8))),
        "cotangent": scatter_about(arg_keys[1], (WINDOWS, LENGTH, D), 1.0, 6.0, ((0, 4), (1, 8))),
        "group_ids": touch_ends(ranked(arg_keys[2], (WINDOWS,), GROUPS, 2), jax.random.fold_in(arg_keys[2], 3), 0, GROUPS - 1).astype(jnp.int32),
        "random_blocks": draw_random_blocks(jax.random.fold_in(arg_keys[19], 71), 0),
        "norm1_gain": jnp.clip(1.0 + 0.15 * jax.random.normal(arg_keys[4], (D,), jnp.float32), 0.25, 1.75),
        "norm1_bias": scatter_about(arg_keys[5], (D,), 0.2, 1.25, (), jnp.float32),
        "query_weight": scatter_about(arg_keys[6], (D, D), D ** -0.5, 0.21875),
        "query_bias": scatter_about(arg_keys[7], (D,), 0.2, 1.25, (), jnp.float32),
        "key_weight": scatter_about(arg_keys[8], (D, D), D ** -0.5, 0.21875),
        "value_weight": scatter_about(arg_keys[9], (D, D), D ** -0.5, 0.21875),
        "value_bias": scatter_about(arg_keys[10], (D,), 0.2, 1.25, (), jnp.float32),
        "out_weight": scatter_about(arg_keys[11], (D, D), (D // 64) ** -0.5, 1.75),
        "out_bias": scatter_about(arg_keys[12], (D,), 0.2, 1.25, (), jnp.float32),
        "norm2_gain": jnp.clip(1.0 + 0.15 * jax.random.normal(arg_keys[13], (D,), jnp.float32), 0.25, 1.75),
        "norm2_bias": scatter_about(arg_keys[14], (D,), 0.2, 1.25, (), jnp.float32),
        "up_weight": scatter_about(arg_keys[15], (D, FF), D ** -0.5, 0.21875),
        "up_bias": scatter_about(arg_keys[16], (FF,), 0.2, 1.25, (), jnp.float32),
        "down_weight": scatter_about(arg_keys[17], (FF, D), FF ** -0.5, 0.109375),
        "down_bias": scatter_about(arg_keys[18], (D,), 0.2, 1.25, (), jnp.float32),
    }


epsilon = 1e-05
masked_score = -1e+30
highest = lax.Precision.HIGHEST

@jax.custom_vjp
def low(v):
    return lax.optimization_barrier(v.astype(jnp.bfloat16)).astype(jnp.float32)

@jax.custom_vjp
def low_back(v):
    return v

def low_keep(v):
    return (low(v), None)

def low_pass(kept, grad):
    return (grad,)

def back_keep(v):
    return (v, None)

def back_low(kept, grad):
    return (low(grad),)
low.defvjp(low_keep, low_pass)
low_back.defvjp(back_keep, back_low)

def layer_norm(inputs, gain_row, shift_row):
    centre = inputs - lax.optimization_barrier(jnp.mean(inputs, axis=-1, keepdims=True))
    spread = lax.optimization_barrier(jnp.mean(centre * centre, axis=-1, keepdims=True))
    return centre * lax.rsqrt(spread + epsilon) * gain_row + shift_row

def window_layer(inputs, params, chosen_blocks):
    gain_one, shift_one, weight_query, bias_query, weight_key, weight_value, bias_value, weight_out, bias_out, gain_two, shift_two, weight_up, bias_up, weight_down, bias_down = params
    block_count = LENGTH // BLOCK
    score_scale = HEAD_DIM ** (-0.5)
    normed = low(layer_norm(inputs, gain_one, shift_one))
    queries = low_back(low(jnp.dot(normed, weight_query, precision=highest) + bias_query))
    keys_all = low_back(low(jnp.dot(normed, weight_key, precision=highest)))
    values_all = low_back(low(jnp.dot(normed, weight_value, precision=highest) + bias_value))
    query_blocks = queries.reshape(block_count, BLOCK, HEADS, HEAD_DIM)
    key_blocks = keys_all.reshape(block_count, BLOCK, HEADS, HEAD_DIM)
    value_blocks = values_all.reshape(block_count, BLOCK, HEADS, HEAD_DIM)

    def one_block(element):
        position, chosen = element
        nearby = jnp.stack([position - 1, position, position + 1, position * 0, position * 0 + block_count - 1])
        listed = jnp.clip(jnp.concatenate([nearby, chosen]), 0, block_count - 1)
        usable = jnp.concatenate([jnp.stack([position > 0, position >= 0, position < block_count - 1]), jnp.ones((2 + RAND,), dtype=bool)])
        keep_slot = jnp.repeat(usable, BLOCK)
        block_keys = jnp.take(key_blocks, listed, axis=0).reshape((5 + RAND) * BLOCK, HEADS, HEAD_DIM)
        block_values = jnp.take(value_blocks, listed, axis=0).reshape((5 + RAND) * BLOCK, HEADS, HEAD_DIM)
        block_query = jnp.take(query_blocks, position, axis=0)
        raw_scores = low_back(jnp.einsum('qhd,khd->hqk', block_query, block_keys, precision=highest) * score_scale)
        softmax_out = jax.nn.softmax(jnp.where(keep_slot[None, None, :], raw_scores, masked_score), axis=-1)
        return jnp.einsum('hqk,khd->qhd', low(softmax_out), block_values, precision=highest)
    attended = lax.map(jax.checkpoint(one_block), (jnp.arange(block_count, dtype=jnp.int32), chosen_blocks))
    attended = low_back(low(attended.reshape(LENGTH, D)))
    hidden = inputs + low_back(jnp.dot(attended, weight_out, precision=highest) + bias_out)
    normed_two = low(layer_norm(hidden, gain_two, shift_two))
    pre_act = low_back(jnp.dot(normed_two, weight_up, precision=highest) + bias_up)
    activated = low(jax.nn.gelu(pre_act, approximate=False))
    return hidden + jnp.dot(activated, weight_down, precision=highest) + bias_down

def reference(tokens, cotangent, group_ids, random_blocks, norm1_gain, norm1_bias, query_weight, query_bias, key_weight, value_weight, value_bias, out_weight, out_bias, norm2_gain, norm2_bias, up_weight, up_bias, down_weight, down_bias):
    params = (norm1_gain.astype(jnp.float32), norm1_bias.astype(jnp.float32), query_weight.astype(jnp.float32), query_bias.astype(jnp.float32), key_weight.astype(jnp.float32), value_weight.astype(jnp.float32), value_bias.astype(jnp.float32), out_weight.astype(jnp.float32), out_bias.astype(jnp.float32), norm2_gain.astype(jnp.float32), norm2_bias.astype(jnp.float32), up_weight.astype(jnp.float32), up_bias.astype(jnp.float32), down_weight.astype(jnp.float32), down_bias.astype(jnp.float32))
    membership = (group_ids[:, None] == jnp.arange(GROUPS, dtype=jnp.int32)[None, :]).astype(jnp.float32)
    group_sizes = lax.optimization_barrier(jnp.sum(membership, axis=0))
    window_scale = WINDOWS / (GROUPS * lax.optimization_barrier(jnp.sum(membership * group_sizes[None, :], axis=1)))

    def one_window(running, element):
        window_tokens, window_cot, window_blocks, scale_here = element

        def forward(inputs, weights):
            return window_layer(inputs, weights, window_blocks)
        result, pullback = jax.vjp(forward, window_tokens.astype(jnp.float32), params)
        input_part, weight_parts = pullback(low(window_cot.astype(jnp.float32) * scale_here))
        running = tuple((running_sum + latest for running_sum, latest in zip(running, weight_parts)))
        return (running, (result.astype(jnp.bfloat16), input_part.astype(jnp.bfloat16)))
    initial = tuple((jnp.zeros_like(entry) for entry in params))
    totals, (output, input_grad) = lax.scan(one_window, initial, (tokens, cotangent, random_blocks, window_scale))
    return (output, input_grad, totals[0], totals[1], totals[2], totals[3], totals[4], totals[5], totals[6], totals[7], totals[8], totals[9], totals[10], totals[11], totals[12], totals[13], totals[14])
```

```python
import functools
import math

import jax
import jax.numpy as jnp
from jax import lax
from jax.experimental import pallas as pl
from jax.experimental.pallas import tpu as pltpu
from jax.sharding import PartitionSpec as P

D = 768
HEADS = 12
HEAD_DIM = 64
FF = 3072
BLOCK = 64
RAND = 3
GROUPS = 8
PIECES = 6
ROWS = 1536
STAGES = 9
VEC_ROWS = 16

MESH = pl.DeviceIdType.MESH
VMEM_LIMIT = 60 << 20
epsilon = 1e-05
masked_score = -1e30
score_scale = HEAD_DIM ** (-0.5)
f32 = jnp.float32
bf16 = jnp.bfloat16

whole_vmem = pl.BlockSpec(memory_space=pltpu.VMEM)


def mm(left, right):
    return jnp.dot(left, right, preferred_element_type=f32)


def mm_nt(left, right):
    return lax.dot_general(left, right, (((1,), (1,)), ((), ())), preferred_element_type=f32)


def normalise(v):
    centre = v - jnp.mean(v, axis=-1, keepdims=True)
    rstd = lax.rsqrt(jnp.mean(centre * centre, axis=-1, keepdims=True) + epsilon)
    return centre * rstd, rstd


def norm_back(err, vhat, rstd, gain):
    g = err * gain
    dv = rstd * (
        g - jnp.mean(g, axis=-1, keepdims=True) - vhat * jnp.mean(g * vhat, axis=-1, keepdims=True)
    )
    return dv, jnp.sum(err * vhat, axis=0, keepdims=True), jnp.sum(err, axis=0, keepdims=True)


def plain_call(kernel, outs, scratch=()):
    return pl.pallas_call(
        kernel,
        out_shape=outs,
        scratch_shapes=scratch,
        compiler_params=pltpu.CompilerParams(vmem_limit_bytes=VMEM_LIMIT),
    )


def qkv_kernel(windows, x, gain, shift, wq, bq, wk, wv, bv, qkv, n1_t):
    tokens = x.shape[0] // windows
    vhat, _ = normalise(x[...].astype(f32))
    n1 = (vhat * gain[...] + shift[...]).astype(bf16)
    n1_t[...] = n1.T
    for part, (weight, bias) in enumerate(((wq, bq), (wk, None), (wv, bv))):
        y = mm(n1, weight[...])
        if bias is not None:
            y = y + bias[...]
        y_t = y.astype(bf16).T
        for w in range(windows):
            for h in range(HEADS):
                qkv[w * HEADS + h, part * HEAD_DIM : (part + 1) * HEAD_DIM, :] = y_t[
                    h * HEAD_DIM : (h + 1) * HEAD_DIM, w * tokens : (w + 1) * tokens
                ]
    for p in range(windows * HEADS, qkv.shape[0]):
        qkv[p] = jnp.zeros(qkv.shape[1:], bf16)


def gather_pair(qkv, pair, rows, lanes_t):
    count, tokens = qkv.shape[0], qkv.shape[3]
    for s in range(count):
        lanes_t[:, s * tokens : (s + 1) * tokens] = qkv[s, pair, rows, :]


def query_tile(ref, pair, tile, rows):
    return jnp.concatenate([ref[2 * tile, pair, rows, :], ref[2 * tile + 1, pair, rows, :]], axis=1)


def biased_scores(keys, q_t, bias, pair, lanes):
    length, width = keys.shape[0], q_t.shape[1]
    raw = mm(keys, q_t) * score_scale
    raw = raw.reshape(length // BLOCK, BLOCK // 8, 8, width)
    return (raw + bias[pair, :, :, lanes][:, None]).reshape(length, width)


Q_ROWS, K_ROWS, V_ROWS = (slice(i * HEAD_DIM, (i + 1) * HEAD_DIM) for i in range(3))


def attend_kernel(qkv, bias, out, mass, k_t, v_t):
    count, pairs, _, tokens = qkv.shape
    width = 2 * tokens
    for pair in range(pairs):
        gather_pair(qkv, pair, K_ROWS, k_t)
        gather_pair(qkv, pair, V_ROWS, v_t)
        keys = k_t[...].T

        def one_tile(tile, carry):
            lanes = pl.ds(pl.multiple_of(tile * width, width), width)
            scores = biased_scores(keys, query_tile(qkv, pair, tile, Q_ROWS), bias, pair, lanes)
            top = jnp.max(scores, axis=0, keepdims=True)
            weight = jnp.exp(scores - top)
            total = jnp.sum(weight, axis=0, keepdims=True)
            mass[pair, :, lanes] = top + jnp.log(total)
            probs = (weight * (1.0 / total)).astype(bf16)
            got = mm(v_t[...], probs).astype(bf16)
            out[2 * tile, pair] = got[:, :tokens]
            out[2 * tile + 1, pair] = got[:, tokens:]
            return carry

        lax.fori_loop(0, count // 2, one_tile, 0)


def attend_back_kernel(qkv, bias, mass, grad, out, k_t, v_t, dk, dv):
    count, pairs, _, tokens = qkv.shape
    width = 2 * tokens
    all_rows = slice(0, HEAD_DIM)
    for pair in range(pairs):
        gather_pair(qkv, pair, K_ROWS, k_t)
        gather_pair(qkv, pair, V_ROWS, v_t)
        keys = k_t[...].T
        values = v_t[...].T
        dk[...] = jnp.zeros_like(dk)
        dv[...] = jnp.zeros_like(dv)

        def one_tile(tile, carry):
            lanes = pl.ds(pl.multiple_of(tile * width, width), width)
            q_t = query_tile(qkv, pair, tile, Q_ROWS)
            g_t = query_tile(grad, pair, tile, all_rows)
            scores = biased_scores(keys, q_t, bias, pair, lanes)
            probs = jnp.exp(scores - mass[pair, :, lanes])
            prob_grad = mm(values, g_t)
            row_dot = jnp.sum(probs * prob_grad, axis=0, keepdims=True)
            score_grad = (probs * (prob_grad - row_dot)).astype(bf16)
            dq = (mm(k_t[...], score_grad) * score_scale).astype(bf16)
            out[2 * tile, pair, Q_ROWS, :] = dq[:, :tokens]
            out[2 * tile + 1, pair, Q_ROWS, :] = dq[:, tokens:]
            dk[...] += mm(score_grad, q_t.T)
            dv[...] += mm(probs.astype(bf16), g_t.T)
            return carry

        lax.fori_loop(0, count // 2, one_tile, 0)
        dk_t = (dk[...] * score_scale).astype(bf16).T
        dv_t = dv[...].astype(bf16).T
        for s in range(count):
            out[s, pair, K_ROWS, :] = dk_t[:, s * tokens : (s + 1) * tokens]
            out[s, pair, V_ROWS, :] = dv_t[:, s * tokens : (s + 1) * tokens]


def ffn_kernel(
    windows,
    x,
    att_pairs,
    cot,
    scale,
    wo,
    bo,
    gain,
    shift,
    wup,
    bup,
    wdown,
    bdown,
    y,
    act_t,
    og,
    n2_t,
    pg,
    bg,
    hg,
    do_pairs,
    att_t,
    vec,
):
    tokens = x.shape[0] // windows
    for w in range(windows):
        att_t[:, w * tokens : (w + 1) * tokens] = att_pairs[
            w * HEADS : (w + 1) * HEADS
        ].reshape(D, tokens)
    att = att_t[...].T
    hidden = x[...].astype(f32) + (mm(att, wo[...]) + bo[...])
    vhat, rstd = normalise(hidden)
    n2 = (vhat * gain[...] + shift[...]).astype(bf16)
    n2_t[...] = n2.T
    for w in range(windows):
        rows = slice(w * tokens, (w + 1) * tokens)
        og[rows] = (cot[rows].astype(f32) * scale[w]).astype(bf16)
    out_grad = og[...]
    total = jnp.zeros(hidden.shape, f32)
    err = jnp.zeros(hidden.shape, f32)
    for part in range(FF // D):
        cols = slice(part * D, (part + 1) * D)
        up_part, down_part = wup[:, cols], wdown[cols, :]
        pre = mm(n2, up_part) + bup[:, cols]
        phi = 0.5 * (1.0 + lax.erf(pre * (0.5**0.5)))
        act = (pre * phi).astype(bf16)
        slope = phi + pre * (jnp.exp(-0.5 * pre * pre) * (1.0 / math.sqrt(2.0 * math.pi)))
        act_t[cols, :] = act.T
        total = total + mm(act, down_part)
        grad = (mm_nt(out_grad, down_part) * slope).astype(bf16)
        pg[part] = grad
        vec[8 + part : 9 + part, :] = jnp.sum(grad.astype(f32), axis=0, keepdims=True)
        err = err + mm_nt(grad, up_part)
    y[...] = (hidden + total + bdown[...]).astype(bf16)
    dv, dgain, dshift = norm_back(err, vhat, rstd, gain[...])
    hidden_grad = out_grad.astype(f32) + dv
    hg[...] = hidden_grad
    branch = hidden_grad.astype(bf16)
    bg[...] = branch
    vec[4:5, :] = jnp.sum(branch.astype(f32), axis=0, keepdims=True)
    vec[5:6, :] = dgain
    vec[6:7, :] = dshift
    vec[7:8, :] = jnp.sum(out_grad.astype(f32), axis=0, keepdims=True)
    datt_t = mm_nt(branch, wo[...]).astype(bf16).T
    for w in range(windows):
        do_pairs[w * HEADS : (w + 1) * HEADS] = datt_t[:, w * tokens : (w + 1) * tokens].reshape(
            HEADS, HEAD_DIM, tokens
        )
    for p in range(windows * HEADS, do_pairs.shape[0]):
        do_pairs[p] = jnp.zeros(do_pairs.shape[1:], bf16)


def input_back_kernel(windows, x, gain, grads, hg, wq, wk, wv, dqkv, dx, vec):
    tokens = x.shape[0] // windows
    vhat, rstd = normalise(x[...].astype(f32))
    err = jnp.zeros(vhat.shape, f32)
    for part, weight in enumerate((wq, wk, wv)):
        for w in range(windows):
            grad_t = grads[
                w * HEADS : (w + 1) * HEADS, part * HEAD_DIM : (part + 1) * HEAD_DIM, :
            ].reshape(D, tokens)
            dqkv[part, w * tokens : (w + 1) * tokens, :] = grad_t.T
        grad = dqkv[part]
        err = err + mm_nt(grad, weight[...])
        if part != 1:
            row = 2 + part // 2
            vec[row : row + 1, :] = jnp.sum(grad.astype(f32), axis=0, keepdims=True)
    dv, dgain, dshift = norm_back(err, vhat, rstd, gain[...])
    dx[...] = (hg[...] + dv).astype(bf16)
    vec[0:1, :] = dgain
    vec[1:2, :] = dshift


class Place:
    def __init__(self, layers):
        self.layers = layers
        self.w = lax.axis_index("win")
        self.s = lax.axis_index("seq")
        self.c = lax.rem(self.s, 2)
        self.z = lax.rem(self.s // 2, 4)
        self.layer = self.s // 8
        self.bits = {"a": lax.rem(self.w, 2), "b": self.w // 2}

    def core(self):
        return (self.w, self.s + 1 - 2 * self.c)

    def across(self, axis):
        step = 1 if axis == "a" else 2
        return (self.w + step - 2 * step * self.bits[axis], self.s)

    def along(self, k):
        return (self.w, self.layer * 8 + lax.rem(self.z + k, 4) * 2 + self.c)

    def layer_at(self, k):
        return (self.w, lax.rem(self.layer + k, self.layers) * 8 + self.z * 2 + self.c)

    def peers(self):
        return (
            [self.core(), self.across("a"), self.across("b")]
            + [self.along(k) for k in (1, 2, 3)]
            + [self.layer_at(k) for k in range(1, self.layers)]
        )


def rcopy(src, dst, send, recv, device):
    return pltpu.make_async_remote_copy(
        src, dst, send, recv, device_id=device, device_id_type=MESH
    )


def span(start, size):
    return pl.ds(pl.multiple_of(start, 16), size)


def reduce_piece(place, order, buf, r0, r1, r2, rz, rl, az, send, recv, free):
    c, z = place.c, place.z
    first, second = place.bits[order[0]], place.bits[order[1]]
    half, quarter, eighth, chunk = ROWS // 2, ROWS // 4, ROWS // 8, ROWS // 32
    o0 = c * half
    partners = (place.core(), place.across(order[0]), place.across(order[1]))

    def release(stage):
        pl.semaphore_signal(free.at[stage], inc=1, device_id=partners[stage], device_id_type=MESH)

    cp = rcopy(buf.at[span((1 - c) * half, half)], r0, send.at[0], recv.at[0], place.core())
    cp.start()
    yield
    cp.wait()
    release(0)
    o1, x1 = o0 + first * quarter, o0 + (1 - first) * quarter
    away = span(x1, quarter)
    buf[away] = buf[away] + r0[span((1 - first) * quarter, quarter)]
    cp = rcopy(buf.at[away], r1, send.at[1], recv.at[1], place.across(order[0]))
    cp.start()
    here = span(o1, quarter)
    buf[here] = buf[here] + r0[span(first * quarter, quarter)]
    yield
    cp.wait()
    release(1)
    o2, x2 = o1 + second * eighth, o1 + (1 - second) * eighth
    away = span(x2, eighth)
    buf[away] = buf[away] + r1[span((1 - second) * eighth, eighth)]
    cp = rcopy(buf.at[away], r2, send.at[2], recv.at[2], place.across(order[1]))
    cp.start()
    here = span(o2, eighth)
    buf[here] = buf[here] + r1[span(second * eighth, eighth)]
    yield
    cp.wait()
    release(2)
    here = span(o2, eighth)
    buf[here] = buf[here] + r2[...]

    def chunk_of(k):
        return buf.at[span(o2 + lax.rem(z + k, 4) * chunk, chunk)]

    cps = [
        rcopy(chunk_of(k), rz.at[3 - k], send.at[2 + k], recv.at[6 - k], place.along(k))
        for k in (1, 2, 3)
    ]
    for cp in cps:
        cp.start()
    yield
    for cp in cps:
        cp.wait_send()
    for k in (1, 2, 3):
        rcopy(rz.at[3 - k], rz.at[3 - k], send.at[2 + k], recv.at[6 - k], place.along(k)).wait_recv()
    mine = span(o2 + z * chunk, chunk)
    total = buf[mine].astype(f32)
    for k in range(3):
        total = total + rz[k].astype(f32)
    buf[mine] = total.astype(bf16)
    if place.layers > 1:
        rl[place.layer] = buf[mine]
        cps = [
            rcopy(
                buf.at[mine],
                rl.at[place.layer],
                send.at[11 + k],
                recv.at[11 + place.layers - k],
                place.layer_at(k),
            )
            for k in range(1, place.layers)
        ]
        for cp in cps:
            cp.start()
        for cp in cps:
            cp.wait_send()
        for k in range(1, place.layers):
            slot = rl.at[lax.rem(place.layer + k, place.layers)]
            rcopy(slot, slot, send.at[11 + k], recv.at[11 + k], place.layer_at(k)).wait_recv()
        total = rl[0].astype(f32)
        for k in range(1, place.layers):
            total = total + rl[k].astype(f32)
        buf[mine] = total.astype(bf16)
    cps = [
        rcopy(buf.at[mine], az.at[3 - k], send.at[5 + k], recv.at[9 - k], place.along(k))
        for k in (1, 2, 3)
    ]
    for cp in cps:
        cp.start()
    yield
    for cp in cps:
        cp.wait_send()
    for k in (1, 2, 3):
        slot = az.at[3 - k]
        rcopy(slot, slot, send.at[5 + k], recv.at[9 - k], place.along(k)).wait_recv()
        buf[span(o2 + lax.rem(z + 4 - k, 4) * chunk, chunk)] = az[3 - k]
    for stage, (start, size) in enumerate(((o2, eighth), (o1, quarter), (o0, half))):
        pl.semaphore_wait(free.at[2 - stage], 1)
        held = buf.at[span(start, size)]
        cp = rcopy(held, held, send.at[9 + stage], recv.at[9 + stage], partners[2 - stage])
        cp.start()
        yield
        cp.wait()


def reduce_vectors(place, vec, out, run, got, send, recv):
    run[0] = vec[...]
    for step, device in enumerate((place.core(), place.across("a"), place.across("b"))):
        cp = rcopy(run.at[step], got.at[step], send.at[step], recv.at[step], device)
        cp.start()
        yield
        cp.wait()
        run[step + 1] = run[step] + got[step]
    got[3 + place.z] = run[3]
    cps = [
        rcopy(run.at[3], got.at[3 + place.z], send.at[2 + k], recv.at[6 - k], place.along(k))
        for k in (1, 2, 3)
    ]
    for cp in cps:
        cp.start()
    yield
    for cp in cps:
        cp.wait_send()
    for k in (1, 2, 3):
        slot = got.at[3 + lax.rem(place.z + k, 4)]
        rcopy(slot, slot, send.at[2 + k], recv.at[2 + k], place.along(k)).wait_recv()
    total = got[3]
    for k in range(1, 4):
        total = total + got[3 + k]
    if place.layers > 1:
        run[4] = total
        got[7 + place.layer] = total
        cps = [
            rcopy(
                run.at[4],
                got.at[7 + place.layer],
                send.at[5 + k],
                recv.at[5 + place.layers - k],
                place.layer_at(k),
            )
            for k in range(1, place.layers)
        ]
        for cp in cps:
            cp.start()
        for cp in cps:
            cp.wait_send()
        for k in range(1, place.layers):
            slot = got.at[7 + lax.rem(place.layer + k, place.layers)]
            rcopy(slot, slot, send.at[5 + k], recv.at[5 + k], place.layer_at(k)).wait_recv()
        total = got[7]
        for k in range(1, place.layers):
            total = total + got[7 + k]
    out[...] = total


def grads_kernel(
    layers, act_t, og, n2_t, pg, n1_t, dqkv, att_t, bg, vec, out, vec_out,
    r0, r1, r2, rz, rl, az, send, recv, free, run, got, vec_send, vec_recv,
):
    place = Place(layers)
    barrier = pltpu.get_barrier_semaphore()
    peers = place.peers()
    for peer in peers:
        pl.semaphore_signal(barrier, inc=1, device_id=peer, device_id_type=MESH)
    pl.semaphore_wait(barrier, len(peers))

    def fill(piece, base, left, left_base, right, rows):
        @pl.loop(0, rows // 256)
        def _(i):
            src = span(left_base + i * 256, 256)
            out[piece, span(base + i * 256, 256), :] = mm(left[src, :], right).astype(bf16)

    def compute(piece):
        if piece < 2:
            fill(piece, 0, act_t, piece * ROWS, og[...], ROWS)
        elif piece < 4:
            for j in range(2):
                fill(piece, j * D, n2_t, 0, pg[(piece - 2) * 2 + j], D)
        elif piece == 4:
            for j in range(2):
                fill(piece, j * D, n1_t, 0, dqkv[j], D)
        else:
            fill(piece, 0, n1_t, 0, dqkv[2], D)
            fill(piece, D, att_t, 0, bg[...], D)

    running = [reduce_vectors(place, vec, vec_out, run, got, vec_send, vec_recv)]
    next(running[0])
    for tick in range(PIECES + STAGES):
        fresh = None
        if tick < PIECES:
            compute(tick)
            fresh = reduce_piece(
                place,
                "ab" if tick % 2 == 0 else "ba",
                out.at[tick],
                r0.at[tick],
                r1.at[tick],
                r2.at[tick],
                rz.at[tick],
                rl.at[tick],
                az.at[tick],
                send.at[tick],
                recv.at[tick],
                free.at[tick],
            )
        still = []
        for stream in running:
            if next(stream, True) is None:
                still.append(stream)
        if fresh is not None:
            next(fresh)
            still.append(fresh)
        running = still
    assert not running


def reduce_grads(layers, *operands):
    layer_slots = layers if layers > 1 else 1
    sems = 12 + layers
    return pl.pallas_call(
        functools.partial(grads_kernel, layers),
        out_shape=(
            jax.ShapeDtypeStruct((PIECES, ROWS, D), bf16),
            jax.ShapeDtypeStruct((VEC_ROWS, D), f32),
        ),
        in_specs=[whole_vmem] * 9,
        out_specs=(whole_vmem, whole_vmem),
        scratch_shapes=[
            pltpu.VMEM((PIECES, ROWS // 2, D), bf16),
            pltpu.VMEM((PIECES, ROWS // 4, D), bf16),
            pltpu.VMEM((PIECES, ROWS // 8, D), bf16),
            pltpu.VMEM((PIECES, 3, ROWS // 32, D), bf16),
            pltpu.VMEM((PIECES, layer_slots, ROWS // 32, D), bf16),
            pltpu.VMEM((PIECES, 3, ROWS // 32, D), bf16),
            pltpu.SemaphoreType.DMA((PIECES, sems)),
            pltpu.SemaphoreType.DMA((PIECES, sems)),
            pltpu.SemaphoreType.REGULAR((PIECES, 3)),
            pltpu.VMEM((5, VEC_ROWS, D), f32),
            pltpu.VMEM((7 + layers, VEC_ROWS, D), f32),
            pltpu.SemaphoreType.DMA((6 + layers,)),
            pltpu.SemaphoreType.DMA((6 + layers,)),
        ],
        compiler_params=pltpu.CompilerParams(
            collective_id=0, has_side_effects=True, vmem_limit_bytes=VMEM_LIMIT
        ),
    )(*operands)


def bias_table(random_blocks, blocks, windows_of):
    query = jnp.arange(blocks)[None, :]
    key = jnp.arange(blocks)[:, None]
    fixed = (
        ((key == query - 1) & (query > 0)).astype(f32)
        + (key == query)
        + ((key == query + 1) & (query < blocks - 1))
        + (key == 0)
        + (key == blocks - 1)
    )
    mine = windows_of[:, None, None, None] == jnp.arange(random_blocks.shape[0])[None, :, None, None]
    random_blocks = jnp.sum(jnp.where(mine, random_blocks[None], 0), axis=1)
    picks = jnp.sum(random_blocks[:, None, :, :] == key[None, :, :, None], axis=3)
    count = fixed[None] + picks.astype(f32)
    bias = jnp.where(count > 0, jnp.log(jnp.maximum(count, 1.0)), masked_score)
    bias = jnp.repeat(bias, BLOCK, axis=2)
    return jnp.broadcast_to(bias[:, :, None, :], bias.shape[:2] + (8, bias.shape[2]))


def body(
    tokens,
    cotangent,
    group_ids,
    random_blocks,
    norm1_gain,
    norm1_bias,
    query_weight,
    query_bias,
    key_weight,
    value_weight,
    value_bias,
    out_weight,
    out_bias,
    norm2_gain,
    norm2_bias,
    up_weight,
    up_bias,
    down_weight,
    down_bias,
):
    seq_count = lax.axis_size("seq")
    seq_index = lax.axis_index("seq")
    windows, here, _ = tokens.shape
    length = here * seq_count
    blocks = length // BLOCK
    rows = windows * here
    pairs = -(-windows * HEADS // seq_count)
    slots = pairs * seq_count
    layers = seq_count // 8
    struct = jax.ShapeDtypeStruct

    membership = (group_ids[:, None] == jnp.arange(GROUPS)[None, :]).astype(f32)
    group_sizes = lax.psum(jnp.sum(membership, axis=0), "win")
    window_total = windows * lax.axis_size("win")
    window_scale = window_total / (GROUPS * jnp.sum(membership * group_sizes[None, :], axis=1))

    windows_of = jnp.minimum((seq_index * pairs + jnp.arange(pairs)) // HEADS, windows - 1)
    bias = bias_table(random_blocks, blocks, windows_of)

    def row(v):
        return v.reshape(1, -1)

    x = tokens.reshape(rows, D)
    qkv, n1_t = plain_call(
        functools.partial(qkv_kernel, windows),
        (struct((slots, 3 * HEAD_DIM, here), bf16), struct((D, rows), bf16)),
    )(
        x,
        row(norm1_gain),
        row(norm1_bias),
        query_weight,
        row(query_bias),
        key_weight,
        value_weight,
        row(value_bias),
    )

    def exchange(v):
        v = v.reshape((seq_count, -1) + v.shape[-1:])
        return lax.all_to_all(v, "seq", split_axis=0, concat_axis=0, tiled=True)

    by_head = exchange(qkv).reshape(seq_count, pairs, 3 * HEAD_DIM, here)
    half_lanes = pltpu.VMEM((HEAD_DIM, length), bf16)
    summed = pltpu.VMEM((length, HEAD_DIM), f32)
    attended, mass = plain_call(
        attend_kernel,
        (struct((seq_count, pairs, HEAD_DIM, here), bf16), struct((pairs, 1, length), f32)),
        (half_lanes, half_lanes),
    )(by_head, bias)
    att_pairs = exchange(attended).reshape(slots, HEAD_DIM, here)

    y, act_t, og, n2_t, pg, bg, hg, do_pairs, att_t, vec_b = pl.pallas_call(
        functools.partial(ffn_kernel, windows),
        out_shape=(
            struct((rows, D), bf16),
            struct((FF, rows), bf16),
            struct((rows, D), bf16),
            struct((D, rows), bf16),
            struct((FF // D, rows, D), bf16),
            struct((rows, D), bf16),
            struct((rows, D), f32),
            struct((slots, HEAD_DIM, here), bf16),
            struct((D, rows), bf16),
            struct((VEC_ROWS, D), f32),
        ),
        in_specs=[whole_vmem] * 3 + [pl.BlockSpec(memory_space=pltpu.SMEM)] + [whole_vmem] * 8,
        out_specs=(whole_vmem,) * 10,
        compiler_params=pltpu.CompilerParams(vmem_limit_bytes=VMEM_LIMIT),
    )(
        x,
        att_pairs,
        cotangent.reshape(rows, D),
        window_scale,
        out_weight,
        row(out_bias),
        row(norm2_gain),
        row(norm2_bias),
        up_weight,
        row(up_bias),
        down_weight,
        row(down_bias),
    )

    grad_by_head = exchange(do_pairs).reshape(seq_count, pairs, HEAD_DIM, here)
    back = plain_call(
        attend_back_kernel,
        struct((seq_count, pairs, 3 * HEAD_DIM, here), bf16),
        (half_lanes, half_lanes, summed, summed),
    )(by_head, bias, mass, grad_by_head)
    grad_pairs = exchange(back).reshape(slots, 3 * HEAD_DIM, here)

    dqkv, dx, vec_a = plain_call(
        functools.partial(input_back_kernel, windows),
        (struct((3, rows, D), bf16), struct((rows, D), bf16), struct((VEC_ROWS, D), f32)),
    )(x, row(norm1_gain), grad_pairs, hg, query_weight, key_weight, value_weight)
    vec = jnp.concatenate([vec_a[:4], vec_b[4:12], jnp.zeros((4, D), f32)], axis=0)

    sums, vec_sums = reduce_grads(layers, act_t, og, n2_t, pg, n1_t, dqkv, att_t, bg, vec)
    down_grad = sums[0:2].reshape(FF, D).astype(f32)
    up_grad = sums[2:4].reshape(FF // D, D, D).astype(f32)
    up_grad = jnp.transpose(up_grad, (1, 0, 2)).reshape(D, FF)
    query_grad = sums[4, :D].astype(f32)
    key_grad = sums[4, D:].astype(f32)
    value_grad = sums[5, :D].astype(f32)
    out_grad = sums[5, D:].astype(f32)
    return (
        y.reshape(tokens.shape),
        dx.reshape(tokens.shape),
        vec_sums[0],
        vec_sums[1],
        query_grad,
        vec_sums[2],
        key_grad,
        value_grad,
        vec_sums[3],
        out_grad,
        vec_sums[4],
        vec_sums[5],
        vec_sums[6],
        up_grad,
        vec_sums[8:12].reshape(FF),
        down_grad,
        vec_sums[7],
    )


def solution(mesh):
    split = P("win", "seq", None)
    return jax.shard_map(
        body,
        mesh=mesh,
        in_specs=(split, split, P("win"), P("win", None, None)) + (P(),) * 15,
        out_specs=(split, split) + (P(),) * 15,
        check_vma=False,
    )
```

```python
import functools
import math

import jax
import jax.numpy as jnp
from jax import lax
from jax.experimental import pallas as pl
from jax.experimental.pallas import tpu as pltpu
from jax.sharding import PartitionSpec as P

D = 768
HEADS = 12
HEAD_DIM = 64
FF = 3072
BLOCK = 64
RAND = 3
GROUPS = 8
TILES = FF // D
VEC_ROWS = 16
OWN = 6
HALF = D // 2

MESH = pl.DeviceIdType.MESH
VMEM_LIMIT = 60 << 20
epsilon = 1e-05
masked_score = -1e30
score_scale = HEAD_DIM ** (-0.5)
f32 = jnp.float32
bf16 = jnp.bfloat16

in_vmem = pl.BlockSpec(memory_space=pltpu.VMEM)
in_smem = pl.BlockSpec(memory_space=pltpu.SMEM)
anywhere = pl.BlockSpec(memory_space=pl.ANY)


def mm(left, right):
    return jnp.dot(left, right, preferred_element_type=f32)


def mm_nt(left, right):
    return lax.dot_general(left, right, (((1,), (1,)), ((), ())), preferred_element_type=f32)


def row(ref):
    return ref[...].reshape(1, -1)


def normalise(v):
    centre = v - jnp.mean(v, axis=-1, keepdims=True)
    rstd = lax.rsqrt(jnp.mean(centre * centre, axis=-1, keepdims=True) + epsilon)
    return centre * rstd, rstd


def norm_back(err, vhat, rstd, gain):
    g = err * gain
    dv = rstd * (
        g - jnp.mean(g, axis=-1, keepdims=True) - vhat * jnp.mean(g * vhat, axis=-1, keepdims=True)
    )
    return dv, jnp.sum(err * vhat, axis=0, keepdims=True), jnp.sum(err, axis=0, keepdims=True)


def rcopy(src, dst, send, recv, device):
    return pltpu.make_async_remote_copy(
        src, dst, send, recv, device_id=device, device_id_type=MESH
    )


def span(start, size):
    return pl.ds(pl.multiple_of(start, 16), size)


class Place:
    def __init__(self, wins, seqs):
        self.wins, self.seqs = wins, seqs
        self.layers = seqs // 8
        self.w = lax.axis_index("win")
        self.s = lax.axis_index("seq")
        self.c = lax.rem(self.s, 2)
        self.z = lax.rem(self.s // 2, 4)
        self.layer = self.s // 8
        self.bits = {"a": lax.rem(self.w, 2), "b": self.w // 2}

    def core(self):
        return (self.w, self.s + 1 - 2 * self.c)

    def across(self, axis):
        step = 1 if axis == "a" else 2
        return (self.w + step - 2 * step * self.bits[axis], self.s)

    def along(self, k):
        return (self.w, self.layer * 8 + lax.rem(self.z + k, 4) * 2 + self.c)

    def layer_at(self, k):
        return (self.w, lax.rem(self.layer + k, self.layers) * 8 + self.z * 2 + self.c)

    def seq_at(self, k):
        return lax.rem(self.s + k, self.seqs)

    def win_at(self, k):
        return (lax.rem(self.w + k, self.wins), self.s)

    def greet(self, across_win):
        barrier = pltpu.get_barrier_semaphore()

        def one(k, carry):
            pl.semaphore_signal(
                barrier, inc=1, device_id=(self.w, self.seq_at(k)), device_id_type=MESH
            )
            return carry

        lax.fori_loop(1, self.seqs, one, 0)
        for peer in across_win:
            pl.semaphore_signal(barrier, inc=1, device_id=peer, device_id_type=MESH)
        return barrier, self.seqs - 1 + len(across_win)


class Exchange:
    def __init__(self, place, pairs, out, into, send, recv):
        self.place, self.pairs = place, pairs
        self.out, self.into, self.send, self.recv = out, into, send, recv

    def copy(self, k, pair):
        place = self.place
        target = place.seq_at(k)
        return rcopy(
            self.out.at[target * self.pairs + pair],
            self.into.at[place.s, pair],
            self.send.at[k, pair],
            self.recv.at[k, pair],
            (place.w, target),
        )

    def start(self, pair):
        def one(k, carry):
            self.copy(k, pair).start()
            return carry

        lax.fori_loop(1, self.place.seqs, one, 0)
        self.into[self.place.s, pair] = self.out[self.place.s * self.pairs + pair]

    def arrived(self, pair):
        def one(k, carry):
            place = self.place
            slot = self.into.at[lax.rem(place.s + place.seqs - k, place.seqs), pair]
            rcopy(
                slot, slot, self.send.at[k, pair], self.recv.at[k, pair], (place.w, place.seq_at(k))
            ).wait_recv()
            return carry

        lax.fori_loop(1, self.place.seqs, one, 0)

    def sent(self, pair):
        def one(k, carry):
            self.copy(k, pair).wait_send()
            return carry

        lax.fori_loop(1, self.place.seqs, one, 0)


Q_ROWS, K_ROWS, V_ROWS = (slice(i * HEAD_DIM, (i + 1) * HEAD_DIM) for i in range(3))


def tile_width(length):
    return 256 if length <= 2048 else 128


def block_ones(keys_t, blocks):
    rows, length = keys_t.shape
    shape = (rows - HEAD_DIM, length)
    part = lax.broadcasted_iota(jnp.int32, shape, 0)
    block = lax.broadcasted_iota(jnp.int32, shape, 1) // BLOCK
    hit = (part == block) | (part == block + blocks) | (part == block + 2 * blocks)
    keys_t[HEAD_DIM:, :] = jnp.where(hit, 1.0, 0.0).astype(bf16)


def gather_rows(ref, pair, rows, into):
    tokens = ref.shape[3]
    for s in range(ref.shape[0]):
        into[: rows.stop - rows.start, s * tokens : (s + 1) * tokens] = ref[s, pair, rows, :]


def query_tile(ref, pair, tile, rows, width):
    parts = width // ref.shape[3]
    return jnp.concatenate([ref[parts * tile + i, pair, rows, :] for i in range(parts)], axis=1)


def put_tile(ref, pair, tile, rows, value, slot):
    tokens = value.shape[1]
    tokens = ref.shape[-1]
    parts = value.shape[1] // tokens
    for i in range(parts):
        ref[slot(parts * tile + i, pair) + (rows,)] = value[:, i * tokens : (i + 1) * tokens]


def biased_scores(keys, q_t, bias, pair, lanes):
    return mm(keys, jnp.concatenate([q_t, bias[pair, :, lanes]], axis=0))


def attend_pair(pair, qkv, bias, keys_t, v_t, put, mass):
    length = v_t.shape[1]
    width = tile_width(length)
    gather_rows(qkv, pair, K_ROWS, keys_t)
    gather_rows(qkv, pair, V_ROWS, v_t)
    keys = keys_t[...].T

    def one_tile(tile, carry):
        lanes = pl.ds(pl.multiple_of(tile * width, width), width)
        scores = biased_scores(keys, query_tile(qkv, pair, tile, Q_ROWS, width), bias, pair, lanes)
        top = jnp.max(scores, axis=0, keepdims=True)
        weight = jnp.exp(scores - top)
        total = jnp.sum(weight, axis=0, keepdims=True)
        mass[pair, :, lanes] = top + jnp.log(total)
        probs = (weight * (1.0 / total)).astype(bf16)
        put(tile, pair, mm(v_t[...], probs).astype(bf16))
        return carry

    lax.fori_loop(0, length // width, one_tile, 0)


def attend_pair_back(pair, qkv, grad, bias, mass, keys_t, v_t, dk, dv, put, finish):
    length = v_t.shape[1]
    width = tile_width(length)
    gather_rows(qkv, pair, K_ROWS, keys_t)
    gather_rows(qkv, pair, V_ROWS, v_t)
    keys = keys_t[...].T
    values = v_t[...].T
    dk[...] = jnp.zeros_like(dk)
    dv[...] = jnp.zeros_like(dv)

    def one_tile(tile, carry):
        lanes = pl.ds(pl.multiple_of(tile * width, width), width)
        q_t = query_tile(qkv, pair, tile, Q_ROWS, width)
        g_t = query_tile(grad, pair, tile, slice(0, HEAD_DIM), width)
        scores = biased_scores(keys, q_t, bias, pair, lanes)
        probs = jnp.exp(scores - mass[pair, :, lanes])
        prob_grad = mm(values, g_t)
        row_dot = jnp.sum(probs * prob_grad, axis=0, keepdims=True)
        score_grad = (probs * (prob_grad - row_dot)).astype(bf16)
        put(tile, pair, (mm(keys_t[:HEAD_DIM, :], score_grad) * score_scale).astype(bf16))
        dk[...] += mm(score_grad, q_t.T)
        dv[...] += mm(probs.astype(bf16), g_t.T)
        return carry

    lax.fori_loop(0, length // width, one_tile, 0)
    finish(pair, dk[...].astype(bf16).T, dv[...].astype(bf16).T)


def project_qkv(x, gain, shift, wq, bq, wk, wv, bv, out, n1_t, windows):
    tokens = x.shape[0] // windows
    vhat, _ = normalise(x[...].astype(f32))
    n1 = (vhat * row(gain) + row(shift)).astype(bf16)
    n1_t[...] = n1.T
    for part, (weight, bias) in enumerate(((wq, bq), (wk, None), (wv, bv))):
        y = mm(n1, weight[...])
        if bias is not None:
            y = y + row(bias)
        y = y.astype(bf16)
        if part == 0:
            y = y * jnp.asarray(score_scale, bf16)
        y_t = y.T
        for w in range(windows):
            for h in range(HEADS):
                out[w * HEADS + h, part * HEAD_DIM : (part + 1) * HEAD_DIM, :] = y_t[
                    h * HEAD_DIM : (h + 1) * HEAD_DIM, w * tokens : (w + 1) * tokens
                ]
    for p in range(windows * HEADS, out.shape[0]):
        out[p] = jnp.zeros(out.shape[1:], bf16)


def feed_forward(
    x, att_t, cot, scales, wo, bo, gain, shift, wup, bup, wdown, bdown,
    y, act_t, og, n2_t, pg, bg, hg, do_out, vec,
):
    windows = len(scales)
    tokens = x.shape[0] // windows
    hidden = x[...].astype(f32) + (mm(att_t[...].T, wo[...]) + row(bo))
    vhat, rstd = normalise(hidden)
    n2 = (vhat * row(gain) + row(shift)).astype(bf16)
    n2_t[...] = n2.T
    for w in range(windows):
        rows = slice(w * tokens, (w + 1) * tokens)
        og[rows] = (cot[rows].astype(f32) * scales[w]).astype(bf16)
    out_grad = og[...]
    total = jnp.zeros(hidden.shape, f32)
    err = jnp.zeros(hidden.shape, f32)
    up_bias = row(bup)
    for part in range(TILES):
        cols = slice(part * D, (part + 1) * D)
        up_part, down_part = wup[:, cols], wdown[cols, :]
        pre = mm(n2, up_part) + up_bias[:, cols]
        phi = 0.5 * (1.0 + lax.erf(pre * (0.5**0.5)))
        act = (pre * phi).astype(bf16)
        slope = phi + pre * (jnp.exp(-0.5 * pre * pre) * (1.0 / math.sqrt(2.0 * math.pi)))
        act_t[part] = act.T
        total = total + mm(act, down_part)
        grad = (mm_nt(out_grad, down_part) * slope).astype(bf16)
        pg[part] = grad
        vec[8 + part : 9 + part, :] = jnp.sum(grad.astype(f32), axis=0, keepdims=True)
        err = err + mm_nt(grad, up_part)
    y[...] = (hidden + total + row(bdown)).astype(bf16)
    dv, dgain, dshift = norm_back(err, vhat, rstd, row(gain))
    hidden_grad = out_grad.astype(f32) + dv
    hg[...] = hidden_grad
    branch = hidden_grad.astype(bf16)
    bg[...] = branch
    vec[4:5, :] = jnp.sum(branch.astype(f32), axis=0, keepdims=True)
    vec[5:6, :] = dgain
    vec[6:7, :] = dshift
    vec[7:8, :] = jnp.sum(out_grad.astype(f32), axis=0, keepdims=True)
    vec[0:4, :] = jnp.zeros((4, D), f32)
    vec[12:16, :] = jnp.zeros((4, D), f32)
    datt_t = mm_nt(branch, wo[...]).astype(bf16).T
    for w in range(windows):
        do_out[w * HEADS : (w + 1) * HEADS] = datt_t[:, w * tokens : (w + 1) * tokens].reshape(
            HEADS, HEAD_DIM, tokens
        )
    for p in range(windows * HEADS, do_out.shape[0]):
        do_out[p] = jnp.zeros(do_out.shape[1:], bf16)


def forward_kernel(
    dims,
    ids, x, gain1, shift1, wq, bq, wk, wv, bv, bias, cot_hbm, wo_hbm, bo, gain2, shift2,
    wup_hbm, bup, wdown_hbm, bdown,
    y, by_head, mass, act_t, og, n2_t, pg, bg, hg, do_out, att_t, n1_t, vec,
    qkv_out, att_out, att_in, keys_t, v_t, counts, cot, wo, wup, wdown,
    load, qkv_send, qkv_recv, att_send, att_recv, count_send, count_recv,
):
    wins, seqs, windows, pairs = dims
    place = Place(wins, seqs)
    loads = [
        pltpu.make_async_copy(src, dst, load.at[i])
        for i, (src, dst) in enumerate(
            ((wo_hbm, wo), (cot_hbm, cot), (wup_hbm, wup), (wdown_hbm, wdown))
        )
    ]
    for copy in loads:
        copy.start()
    barrier, expected = place.greet([place.win_at(k) for k in range(1, wins)])
    project_qkv(x, gain1, shift1, wq, bq, wk, wv, bv, qkv_out, n1_t, windows)
    lane = lax.broadcasted_iota(jnp.int32, (8, 128), 1)
    member = [(lane == ids[w]).astype(f32) for w in range(windows)]
    counts[place.w] = sum(member[1:], member[0])
    pl.semaphore_wait(barrier, expected)

    qkv_moves = Exchange(place, pairs, qkv_out, by_head, qkv_send, qkv_recv)
    for pair in range(pairs):
        qkv_moves.start(pair)
    mine = counts.at[place.w]
    count_moves = [
        rcopy(mine, mine, count_send.at[k], count_recv.at[k], place.win_at(k))
        for k in range(1, wins)
    ]
    for copy in count_moves:
        copy.start()

    block_ones(keys_t, v_t.shape[1] // BLOCK)
    att_moves = Exchange(place, pairs, att_out, att_in, att_send, att_recv)

    def put(tile, pair, value):
        tokens = att_out.shape[-1]
        parts = value.shape[1] // tokens
        for i in range(parts):
            att_out[(tile * parts + i) * pairs + pair] = value[:, i * tokens : (i + 1) * tokens]

    for pair in range(pairs):
        qkv_moves.arrived(pair)
        attend_pair(pair, by_head, bias, keys_t, v_t, put, mass)
        att_moves.start(pair)

    for copy in count_moves:
        copy.wait_send()
    for k in range(1, wins):
        slot = counts.at[lax.rem(place.w + wins - k, wins)]
        rcopy(slot, slot, count_send.at[k], count_recv.at[k], place.win_at(k)).wait_recv()
    sizes = counts[0]
    for k in range(1, wins):
        sizes = sizes + counts[k]
    first_row = lax.broadcasted_iota(jnp.int32, (8, 128), 0) == 0
    scales = []
    for w in range(windows):
        own_size = jnp.sum(jnp.where(first_row, member[w] * sizes, 0.0), keepdims=True)
        scales.append(windows * wins / (GROUPS * own_size))

    for pair in range(pairs):
        att_moves.arrived(pair)
    tokens = x.shape[0] // windows
    for w in range(windows):
        for h in range(HEADS):
            slot, pair = divmod(w * HEADS + h, pairs)
            att_t[h * HEAD_DIM : (h + 1) * HEAD_DIM, w * tokens : (w + 1) * tokens] = att_in[
                slot, pair
            ]
    for copy in loads:
        copy.wait()
    feed_forward(
        x, att_t, cot, scales, wo, bo, gain2, shift2, wup, bup, wdown, bdown,
        y, act_t, og, n2_t, pg, bg, hg, do_out, vec,
    )
    for pair in range(pairs):
        qkv_moves.sent(pair)
        att_moves.sent(pair)


def reduce_halves(place, out, index, j, r1, r2, rz, rl, az, send, recv, free):
    parts = [
        reduce_half(
            place, order, out.at[index], h * HALF,
            *(ref.at[2 * j + h] for ref in (r1, r2, rz, rl, az, send, recv, free)),
        )
        for h, order in enumerate(("ab", "ba"))
    ]
    while True:
        alive = [next(part, True) is None for part in parts]
        if not any(alive):
            break
        yield
    held = out.at[index]
    cp = rcopy(held, held, send.at[2 * j, 8], recv.at[2 * j, 8], place.core())
    cp.start()
    yield
    cp.wait()


def reduce_half(place, order, buf, col, r1, r2, rz, rl, az, send, recv, free):
    z = place.z
    cols = pl.ds(col, HALF)
    first, second = place.bits[order[0]], place.bits[order[1]]
    quarter, eighth, chunk = D // 2, D // 4, D // 16
    partners = (place.across(order[0]), place.across(order[1]))

    def at(start, size):
        return buf.at[span(start, size), cols]

    def release(stage):
        pl.semaphore_signal(free.at[stage], inc=1, device_id=partners[stage], device_id_type=MESH)

    o1, x1 = first * quarter, (1 - first) * quarter
    cp = rcopy(at(x1, quarter), r1, send.at[0], recv.at[0], partners[0])
    cp.start()
    yield
    cp.wait()
    release(0)
    o2, x2 = o1 + second * eighth, o1 + (1 - second) * eighth
    at(x2, eighth)[...] = at(x2, eighth)[...] + r1[span((1 - second) * eighth, eighth)]
    cp = rcopy(at(x2, eighth), r2, send.at[1], recv.at[1], partners[1])
    cp.start()
    at(o2, eighth)[...] = at(o2, eighth)[...] + r1[span(second * eighth, eighth)]
    yield
    cp.wait()
    release(1)
    at(o2, eighth)[...] = at(o2, eighth)[...] + r2[...]

    def chunk_of(k):
        return at(o2 + lax.rem(z + k, 4) * chunk, chunk)

    cps = [
        rcopy(chunk_of(k), rz.at[3 - k], send.at[1 + k], recv.at[5 - k], place.along(k))
        for k in (1, 2, 3)
    ]
    for cp in cps:
        cp.start()
    yield
    for cp in cps:
        cp.wait_send()
    for k in (1, 2, 3):
        rcopy(rz.at[3 - k], rz.at[3 - k], send.at[1 + k], recv.at[5 - k], place.along(k)).wait_recv()
    mine = at(o2 + z * chunk, chunk)
    total = mine[...].astype(f32)
    for k in range(3):
        total = total + rz[k].astype(f32)
    mine[...] = total.astype(bf16)
    layers = place.layers
    if layers > 1:
        rl[place.layer] = mine[...]
        cps = [
            rcopy(
                mine, rl.at[place.layer], send.at[10 + k], recv.at[10 + layers - k],
                place.layer_at(k),
            )
            for k in range(1, layers)
        ]
        for cp in cps:
            cp.start()
        for cp in cps:
            cp.wait_send()
        for k in range(1, layers):
            slot = rl.at[lax.rem(place.layer + k, layers)]
            rcopy(slot, slot, send.at[10 + k], recv.at[10 + k], place.layer_at(k)).wait_recv()
        total = rl[0].astype(f32)
        for k in range(1, layers):
            total = total + rl[k].astype(f32)
        mine[...] = total.astype(bf16)
    cps = [
        rcopy(mine, az.at[3 - k], send.at[4 + k], recv.at[8 - k], place.along(k)) for k in (1, 2, 3)
    ]
    for cp in cps:
        cp.start()
    yield
    for cp in cps:
        cp.wait_send()
    for k in (1, 2, 3):
        slot = az.at[3 - k]
        rcopy(slot, slot, send.at[4 + k], recv.at[8 - k], place.along(k)).wait_recv()
        at(o2 + lax.rem(z + 4 - k, 4) * chunk, chunk)[...] = slot[...]
    for stage, start, size in ((1, o2, eighth), (0, o1, quarter)):
        pl.semaphore_wait(free.at[stage], 1)
        held = at(start, size)
        cp = rcopy(held, held, send.at[10 - stage], recv.at[10 - stage], partners[stage])
        cp.start()
        yield
        cp.wait()


def reduce_vectors(place, out, run, got, send, recv):
    for step, device in enumerate((place.core(), place.across("a"), place.across("b"))):
        cp = rcopy(run.at[step], got.at[step], send.at[step], recv.at[step], device)
        cp.start()
        yield
        cp.wait()
        run[step + 1] = run[step] + got[step]
    got[3 + place.z] = run[3]
    cps = [
        rcopy(run.at[3], got.at[3 + place.z], send.at[2 + k], recv.at[6 - k], place.along(k))
        for k in (1, 2, 3)
    ]
    for cp in cps:
        cp.start()
    yield
    for cp in cps:
        cp.wait_send()
    for k in (1, 2, 3):
        slot = got.at[3 + lax.rem(place.z + k, 4)]
        rcopy(slot, slot, send.at[2 + k], recv.at[2 + k], place.along(k)).wait_recv()
    total = got[3]
    for k in range(1, 4):
        total = total + got[3 + k]
    layers = place.layers
    if layers > 1:
        run[4] = total
        got[7 + place.layer] = total
        cps = [
            rcopy(
                run.at[4], got.at[7 + place.layer], send.at[5 + k], recv.at[5 + layers - k],
                place.layer_at(k),
            )
            for k in range(1, layers)
        ]
        for cp in cps:
            cp.start()
        for cp in cps:
            cp.wait_send()
        for k in range(1, layers):
            slot = got.at[7 + lax.rem(place.layer + k, layers)]
            rcopy(slot, slot, send.at[5 + k], recv.at[5 + k], place.layer_at(k)).wait_recv()
        total = got[7]
        for k in range(1, layers):
            total = total + got[7 + k]
    out[...] = total


def input_back(x, gain, grad_in, hg, wq, wk, wv, rhs, dx, vec, windows, pairs):
    tokens = x.shape[0] // windows
    vhat, rstd = normalise(x[...].astype(f32))
    err = jnp.zeros(vhat.shape, f32)
    for part, weight in enumerate((wq, wk, wv)):
        rows = slice(part * HEAD_DIM, (part + 1) * HEAD_DIM)
        for w in range(windows):
            slots = [divmod(w * HEADS + h, pairs) for h in range(HEADS)]
            grad_t = jnp.concatenate([grad_in[s, p, rows, :] for s, p in slots], axis=0)
            rhs[part, w * tokens : (w + 1) * tokens, :] = grad_t.T
        grad = rhs[part]
        err = err + mm_nt(grad, weight[...])
        if part != 1:
            r = 2 + part // 2
            vec[r : r + 1, :] = jnp.sum(grad.astype(f32), axis=0, keepdims=True)
    dv, dgain, dshift = norm_back(err, vhat, rstd, row(gain))
    dx[...] = (hg[...] + dv).astype(bf16)
    vec[0:1, :] = dgain
    vec[1:2, :] = dshift


def backward_kernel(
    dims,
    x, gain1, by_head, bias, mass, do_out, act_t, og, n2_t, pg, bg, hg, att_t, n1_t, vec,
    wq_hbm, wk_hbm, wv_hbm,
    dx, out, vec_out,
    wq, wk, wv, do_in, dqkv_out, dqkv_in, keys_t, v_t, dk, dv, lhs, rhs,
    s_act, s_pg, s_og, s_n2, s_lhs, s_rhs,
    r1, r2, rz, rl, az, run, got,
    load, send, recv, free, do_send, do_recv, dqkv_send, dqkv_recv, core_send, core_recv,
    vec_send, vec_recv,
):
    wins, seqs, windows, pairs = dims
    place = Place(wins, seqs)
    c = place.c
    loads = [
        pltpu.make_async_copy(src, dst, load.at[i])
        for i, (src, dst) in enumerate(((wq_hbm, wq), (wk_hbm, wk), (wv_hbm, wv)))
    ]
    for copy in loads:
        copy.start()
    others = [place.layer_at(k) for k in range(1, place.layers)]
    barrier, expected = place.greet([place.across("a"), place.across("b")])
    pl.semaphore_wait(barrier, expected)

    do_moves = Exchange(place, pairs, do_out, do_in, do_send, do_recv)
    dqkv_moves = Exchange(place, pairs, dqkv_out, dqkv_in, dqkv_send, dqkv_recv)
    for pair in range(pairs):
        do_moves.start(pair)

    core_count = [0]

    def to_core(src, dst):
        i = core_count[0]
        core_count[0] += 1
        cp = rcopy(src, dst, core_send.at[i], core_recv.at[i], place.core())
        cp.start()
        return cp

    theirs = 2 * (1 - c)
    first_moves = [to_core(og, s_og)]
    first_moves += [to_core(act_t.at[theirs + i], s_act.at[i]) for i in range(2)]
    second_moves = [to_core(n2_t, s_n2)]
    second_moves += [to_core(pg.at[theirs + i], s_pg.at[i]) for i in range(2)]
    lhs[0] = n1_t[...]
    lhs[1] = att_t[...]
    rhs[3] = bg[...]
    lhs_moves = [to_core(lhs.at[i], s_lhs.at[i]) for i in range(2)]
    block_ones(keys_t, v_t.shape[1] // BLOCK)

    def fill(index, parts):
        @pl.loop(0, D // 256)
        def _(i):
            rows = span(i * 256, 256)
            (left, right), (left2, right2) = parts
            out[index, rows, :] = (mm(left[rows, :], right[...]) + mm(left2[rows, :], right2[...])).astype(bf16)

    def stream(j):
        index = (j // 2) * 4 + 2 * c + j % 2
        if j < 2:
            parts = ((act_t.at[2 * c + j], og), (s_act.at[j], s_og))
        elif j < 4:
            parts = ((n2_t, pg.at[2 * c + j - 2]), (s_n2, s_pg.at[j - 2]))
        else:
            use_att = c * (j % 2)
            parts = (
                (lhs.at[use_att], rhs.at[2 * c + j % 2]),
                (s_lhs.at[use_att], s_rhs.at[j % 2]),
            )
        fill(index, parts)
        return reduce_halves(place, out, index, j, r1, r2, rz, rl, az, send, recv, free)

    running = []

    def begin(j):
        running.append(stream(j))
        next(running[-1])

    def tick():
        running[:] = [one for one in running if next(one, True) is None]

    for copy in first_moves:
        copy.wait()
    begin(0)
    for copy in second_moves:
        copy.wait()

    def put(tile, pair, value):
        tokens = dqkv_out.shape[-1]
        parts = value.shape[1] // tokens
        for i in range(parts):
            dqkv_out[(tile * parts + i) * pairs + pair, Q_ROWS, :] = value[
                :, i * tokens : (i + 1) * tokens
            ]

    def finish(pair, dk_t, dv_t):
        tokens = dqkv_out.shape[-1]
        for s in range(seqs):
            lanes = slice(s * tokens, (s + 1) * tokens)
            dqkv_out[s * pairs + pair, K_ROWS, :] = dk_t[:, lanes]
            dqkv_out[s * pairs + pair, V_ROWS, :] = dv_t[:, lanes]

    for copy in lhs_moves:
        copy.wait()
    for pair in range(pairs):
        do_moves.arrived(pair)
        tick()
        if pair + 1 < 4:
            begin(pair + 1)
        attend_pair_back(
            pair, by_head, do_in, bias, mass, keys_t, v_t, dk, dv, put, finish
        )
        dqkv_moves.start(pair)
    for j in range(pairs + 1, 4):
        tick()
        begin(j)
    tick()
    for pair in range(pairs):
        dqkv_moves.arrived(pair)
    for copy in loads:
        copy.wait()
    run[0] = vec[...]
    input_back(x, gain1, dqkv_in, hg, wq, wk, wv, rhs, dx, run.at[0], windows, pairs)
    rhs_moves = [to_core(rhs.at[theirs + i], s_rhs.at[i]) for i in range(2)]
    running.append(reduce_vectors(place, vec_out, run, got, vec_send, vec_recv))
    next(running[-1])
    tick()
    for copy in rhs_moves:
        copy.wait()
    begin(4)
    tick()
    begin(5)
    while running:
        tick()
    for pair in range(pairs):
        do_moves.sent(pair)
        dqkv_moves.sent(pair)


def bias_rows(random_blocks, blocks, windows_of, rows):
    query = jnp.arange(blocks)[None, :]
    key = jnp.arange(blocks)[:, None]
    fixed = (
        ((key == query - 1) & (query > 0)).astype(f32)
        + (key == query)
        + ((key == query + 1) & (query < blocks - 1))
        + (key == 0)
        + (key == blocks - 1)
    )
    mine = windows_of[:, None, None, None] == jnp.arange(random_blocks.shape[0])[None, :, None, None]
    chosen = jnp.sum(jnp.where(mine, random_blocks[None], 0), axis=1)
    picks = jnp.sum(chosen[:, None, :, :] == key[None, :, :, None], axis=3)
    count = fixed[None] + picks.astype(f32)
    rest = jnp.where(count > 0, jnp.log(jnp.maximum(count, 1.0)), masked_score)
    terms = []
    for _ in range(3):
        terms.append(lax.reduce_precision(rest, 8, 7))
        rest = jnp.where(count > 0, rest - terms[-1], 0.0)
    table = jnp.concatenate(terms, axis=1)
    table = jnp.pad(table, ((0, 0), (0, rows - 3 * blocks), (0, 0)))
    return jnp.repeat(table.astype(bf16), BLOCK, axis=2)


def body(
    tokens,
    cotangent,
    group_ids,
    random_blocks,
    norm1_gain,
    norm1_bias,
    query_weight,
    query_bias,
    key_weight,
    value_weight,
    value_bias,
    out_weight,
    out_bias,
    norm2_gain,
    norm2_bias,
    up_weight,
    up_bias,
    down_weight,
    down_bias,
):
    seqs, wins = lax.axis_size("seq"), lax.axis_size("win")
    windows, here, _ = tokens.shape
    length = here * seqs
    blocks = length // BLOCK
    rows = windows * here
    pairs = -(-windows * HEADS // seqs)
    slots = pairs * seqs
    layers = seqs // 8
    extra = -(-(HEAD_DIM + 3 * blocks) // 128) * 128 - HEAD_DIM
    dims = (wins, seqs, windows, pairs)
    struct = jax.ShapeDtypeStruct
    dma = pltpu.SemaphoreType.DMA
    vmem = pltpu.VMEM

    first = lax.axis_index("seq") * pairs
    windows_of = jnp.minimum((first + jnp.arange(pairs)) // HEADS, windows - 1)
    bias = bias_rows(random_blocks, blocks, windows_of, extra)
    x = tokens.reshape(rows, D)

    y, by_head, mass, act_t, og, n2_t, pg, bg, hg, do_out, att_t, n1_t, vec = pl.pallas_call(
        functools.partial(forward_kernel, dims),
        out_shape=(
            struct((rows, D), bf16),
            struct((seqs, pairs, 3 * HEAD_DIM, here), bf16),
            struct((pairs, 1, length), f32),
            struct((TILES, D, rows), bf16),
            struct((rows, D), bf16),
            struct((D, rows), bf16),
            struct((TILES, rows, D), bf16),
            struct((rows, D), bf16),
            struct((rows, D), f32),
            struct((slots, HEAD_DIM, here), bf16),
            struct((D, rows), bf16),
            struct((D, rows), bf16),
            struct((VEC_ROWS, D), f32),
        ),
        in_specs=[in_smem]
        + [in_vmem] * 9
        + [anywhere, anywhere]
        + [in_vmem] * 3
        + [anywhere, in_vmem, anywhere, in_vmem],
        out_specs=(in_vmem,) * 13,
        scratch_shapes=[
            vmem((slots, 3 * HEAD_DIM, here), bf16),
            vmem((slots, HEAD_DIM, here), bf16),
            vmem((seqs, pairs, HEAD_DIM, here), bf16),
            vmem((HEAD_DIM + extra, length), bf16),
            vmem((HEAD_DIM, length), bf16),
            vmem((wins, 8, 128), f32),
            vmem((rows, D), bf16),
            vmem((D, D), bf16),
            vmem((D, FF), bf16),
            vmem((FF, D), bf16),
            dma((4,)),
            dma((seqs, pairs)),
            dma((seqs, pairs)),
            dma((seqs, pairs)),
            dma((seqs, pairs)),
            dma((wins,)),
            dma((wins,)),
        ],
        compiler_params=pltpu.CompilerParams(
            collective_id=0, has_side_effects=True, vmem_limit_bytes=VMEM_LIMIT
        ),
    )(
        group_ids, x, norm1_gain, norm1_bias, query_weight, query_bias, key_weight, value_weight,
        value_bias, bias, cotangent.reshape(rows, D), out_weight, out_bias, norm2_gain, norm2_bias,
        up_weight, up_bias, down_weight, down_bias,
    )

    layer_slots = layers if layers > 1 else 1
    halves = 2 * OWN
    dx, sums, vec_sums = pl.pallas_call(
        functools.partial(backward_kernel, dims),
        out_shape=(
            struct((rows, D), bf16),
            struct((2 * OWN, D, D), bf16),
            struct((VEC_ROWS, D), f32),
        ),
        in_specs=[in_vmem] * 15 + [anywhere] * 3,
        out_specs=(in_vmem,) * 3,
        scratch_shapes=[
            vmem((D, D), bf16),
            vmem((D, D), bf16),
            vmem((D, D), bf16),
            vmem((seqs, pairs, HEAD_DIM, here), bf16),
            vmem((slots, 3 * HEAD_DIM, here), bf16),
            vmem((seqs, pairs, 3 * HEAD_DIM, here), bf16),
            vmem((HEAD_DIM + extra, length), bf16),
            vmem((HEAD_DIM, length), bf16),
            vmem((length, HEAD_DIM), f32),
            vmem((length, HEAD_DIM), f32),
            vmem((2, D, rows), bf16),
            vmem((4, rows, D), bf16),
            vmem((2, D, rows), bf16),
            vmem((2, rows, D), bf16),
            vmem((rows, D), bf16),
            vmem((D, rows), bf16),
            vmem((2, D, rows), bf16),
            vmem((2, rows, D), bf16),
            vmem((halves, D // 2, HALF), bf16),
            vmem((halves, D // 4, HALF), bf16),
            vmem((halves, 3, D // 16, HALF), bf16),
            vmem((halves, layer_slots, D // 16, HALF), bf16),
            vmem((halves, 3, D // 16, HALF), bf16),
            vmem((5, VEC_ROWS, D), f32),
            vmem((7 + layers, VEC_ROWS, D), f32),
            dma((3,)),
            dma((halves, 11 + layers)),
            dma((halves, 11 + layers)),
            pltpu.SemaphoreType.REGULAR((halves, 2)),
            dma((seqs, pairs)),
            dma((seqs, pairs)),
            dma((seqs, pairs)),
            dma((seqs, pairs)),
            dma((10,)),
            dma((10,)),
            dma((6 + layers,)),
            dma((6 + layers,)),
        ],
        compiler_params=pltpu.CompilerParams(
            collective_id=1, has_side_effects=True, vmem_limit_bytes=VMEM_LIMIT
        ),
    )(
        x, norm1_gain, by_head, bias, mass, do_out, act_t, og, n2_t, pg, bg, hg, att_t, n1_t, vec,
        query_weight, key_weight, value_weight,
    )

    down_grad = sums[0:4].reshape(FF, D).astype(f32)
    up_grad = jnp.transpose(sums[4:8].astype(f32), (1, 0, 2)).reshape(D, FF)
    query_grad, key_grad, value_grad, out_grad = (sums[8 + i].astype(f32) for i in range(4))
    return (
        y.reshape(tokens.shape),
        dx.reshape(tokens.shape),
        vec_sums[0],
        vec_sums[1],
        query_grad,
        vec_sums[2],
        key_grad,
        value_grad,
        vec_sums[3],
        out_grad,
        vec_sums[4],
        vec_sums[5],
        vec_sums[6],
        up_grad,
        vec_sums[8:12].reshape(FF),
        down_grad,
        vec_sums[7],
    )


def solution(mesh):
    split = P("win", "seq", None)
    return jax.shard_map(
        body,
        mesh=mesh,
        in_specs=(split, split, P("win"), P("win", None, None)) + (P(),) * 15,
        out_specs=(split, split) + (P(),) * 15,
        check_vma=False,
    )
```

```python
import functools
import math

import jax
import jax.numpy as jnp
from jax import lax
from jax.experimental import pallas as pl
from jax.experimental.pallas import tpu as pltpu
from jax.sharding import PartitionSpec as P

D = 768
HEADS = 12
HEAD_DIM = 64
FF = 3072
BLOCK = 64
RAND = 3
GROUPS = 8
TILES = FF // D
VEC_ROWS = 16
OWN = 6
HALF = D // 2
VECTORS = 12
ORDERS = (
    "labh", "balh", "ablh", "balh",
    "ablh", "balh", "ablh", "blah",
    "ablh", "balh", "ablh", "balh",
)
SCHEDULE = (
    "2301AAA23504123765Wv01234vX9876v45ab0v79",
    "184v25630v1a647vb215983026b49a71853260b4",
    "93a178541162722530b963a380047b4594a8655b",
    "a9676b877a898899abaabb",
)

MESH = pl.DeviceIdType.MESH
VMEM_LIMIT = 63 << 20
epsilon = 1e-05
masked_score = -1e30
score_scale = HEAD_DIM ** (-0.5)
f32 = jnp.float32
bf16 = jnp.bfloat16

in_vmem = pl.BlockSpec(memory_space=pltpu.VMEM)
in_smem = pl.BlockSpec(memory_space=pltpu.SMEM)
anywhere = pl.BlockSpec(memory_space=pl.ANY)


def mm(left, right):
    return jnp.dot(left, right, preferred_element_type=f32)


def mm_nt(left, right):
    return lax.dot_general(left, right, (((1,), (1,)), ((), ())), preferred_element_type=f32)


def row(ref):
    return ref[...].reshape(1, -1)


def normalise(v):
    centre = v - jnp.mean(v, axis=-1, keepdims=True)
    rstd = lax.rsqrt(jnp.mean(centre * centre, axis=-1, keepdims=True) + epsilon)
    return centre * rstd, rstd


def norm_back(err, vhat, rstd, gain):
    g = err * gain
    dv = rstd * (
        g - jnp.mean(g, axis=-1, keepdims=True) - vhat * jnp.mean(g * vhat, axis=-1, keepdims=True)
    )
    return dv, jnp.sum(err * vhat, axis=0, keepdims=True), jnp.sum(err, axis=0, keepdims=True)


def rcopy(src, dst, send, recv, device):
    return pltpu.make_async_remote_copy(
        src, dst, send, recv, device_id=device, device_id_type=MESH
    )


def span(start, size):
    return pl.ds(pl.multiple_of(start, 16), size)


class Place:
    def __init__(self, wins, seqs):
        self.wins, self.seqs = wins, seqs
        self.layers = seqs // 8
        self.w = lax.axis_index("win")
        self.s = lax.axis_index("seq")
        self.c = lax.rem(self.s, 2)
        self.z = lax.rem(self.s // 2, 4)
        self.layer = self.s // 8
        self.layer_steps = (seqs // 8).bit_length() - 1
        self.size = seqs // 2
        self.window = self.s // self.size
        self.g = lax.rem(self.s, self.size)
        self.base = self.s - self.g
        self.core_free = None
        self.bits = {"a": lax.rem(self.w, 2), "b": self.w // 2}

    def core(self):
        return (self.w, self.s + 1 - 2 * self.c)

    def across(self, axis):
        step = 1 if axis == "a" else 2
        return (self.w + step - 2 * step * self.bits[axis], self.s)

    def along(self, k):
        return (self.w, self.layer * 8 + lax.rem(self.z + k, 4) * 2 + self.c)

    def layer_swap(self, i):
        step = 2**i
        bit = lax.rem(self.layer // step, 2)
        return (self.w, self.s + 8 * step * (1 - 2 * bit))

    def step_z(self, step):
        bit = lax.rem(self.z // step, 2)
        return (self.w, self.s + 2 * step * (1 - 2 * bit))

    def core_open(self):
        if self.core_free is not None:
            pl.semaphore_wait(self.core_free, 1)
            self.core_free = None

    def group_at(self, k):
        return (self.w, self.base + lax.rem(self.g + k, self.size))

    def partner(self):
        return (self.w, lax.rem(self.s + self.size, self.seqs))

    def win_at(self, k):
        return (lax.rem(self.w + k, self.wins), self.s)

    def greet(self):
        barrier = pltpu.get_barrier_semaphore()

        def one(k, carry):
            pl.semaphore_signal(barrier, inc=1, device_id=self.group_at(k), device_id_type=MESH)
            return carry

        lax.fori_loop(1, self.size, one, 0)
        others = [self.partner()]
        others += [self.win_at(k) for k in range(1, self.wins)]
        others += [self.layer_swap(i) for i in range(self.layer_steps)]
        for peer in others:
            pl.semaphore_signal(barrier, inc=1, device_id=peer, device_id_type=MESH)
        pl.semaphore_wait(barrier, self.size - 1 + len(others))


class Exchange:
    def __init__(self, place, pairs, out, into, send, recv):
        self.place, self.pairs = place, pairs
        self.out, self.into, self.send, self.recv = out, into, send, recv

    def copy(self, k, pair, part, lanes):
        place = self.place
        target = lax.rem(place.g + k, place.size)
        return rcopy(
            self.out.at[target * self.pairs + pair, :, lanes],
            self.into.at[place.g, pair, :, lanes],
            self.send.at[k, pair, part],
            self.recv.at[k, pair, part],
            place.group_at(k),
        )

    def start(self, pair, part=0, lanes=slice(None)):
        def one(k, carry):
            self.copy(k, pair, part, lanes).start()
            return carry

        place = self.place
        lax.fori_loop(1, place.size, one, 0)
        self.into[place.g, pair, :, lanes] = self.out[place.g * self.pairs + pair, :, lanes]

    def arrived(self, pair, part=0, lanes=slice(None)):
        def one(k, carry):
            place = self.place
            slot = self.into.at[lax.rem(place.g + place.size - k, place.size), pair, :, lanes]
            rcopy(
                slot, slot, self.send.at[k, pair, part], self.recv.at[k, pair, part],
                place.group_at(k),
            ).wait_recv()
            return carry

        lax.fori_loop(1, self.place.size, one, 0)

    def sent(self, pair, part=0, lanes=slice(None)):
        def one(k, carry):
            self.copy(k, pair, part, lanes).wait_send()
            return carry

        lax.fori_loop(1, self.place.size, one, 0)


Q_ROWS, K_ROWS, V_ROWS = (slice(i * HEAD_DIM, (i + 1) * HEAD_DIM) for i in range(3))


def tile_width(length):
    return 256 if length <= 2048 else 128


def block_at(place, first, shape, axis):
    index = first + lax.broadcasted_iota(jnp.int32, shape, axis)
    slot, half = index // 256, lax.rem(index // 128, 2)
    window = place.window + half - 2 * half * place.window
    return (window * place.size + slot) * 2 + lax.rem(index // BLOCK, 2)


def block_ones(place, keys, blocks):
    length, lanes = keys.shape

    def one_group(group, carry):
        shape = (256, lanes)
        part = lax.broadcasted_iota(jnp.int32, shape, 1) - HEAD_DIM
        block = block_at(place, group * 256, shape, 0)
        hit = (part == block) | (part == block + blocks) | (part == block + 2 * blocks)
        keys[span(group * 256, 256), :] = jnp.where(hit, 1.0, 0.0).astype(bf16)
        return carry

    lax.fori_loop(0, length // 256, one_group, 0)


def gather_rows(ref, pair, rows, into):
    tokens = ref.shape[3]
    for s in range(ref.shape[0]):
        into[: rows.stop - rows.start, s * tokens : (s + 1) * tokens] = ref[s, pair, rows, :]


def place_of_tile(tile, width):
    per_slot = 256 // width
    if per_slot == 1:
        return tile, slice(None)
    return tile // per_slot, pl.ds(pl.multiple_of(lax.rem(tile, per_slot) * width, width), width)


def biased_scores(keys, q_t, bias, lanes):
    return mm(keys[...], jnp.concatenate([q_t, bias[:, lanes]], axis=0))


def attend_pair(pair, qkv, bias, keys, k_t, v_t, small_out, raw, mass):
    length = v_t.shape[1]
    pairs = qkv.shape[1]
    width = tile_width(length)
    step = length if length <= 1024 else 512
    gather_rows(qkv, pair, K_ROWS, k_t)
    gather_rows(qkv, pair, V_ROWS, v_t)
    keys[:, :HEAD_DIM] = k_t[...].T

    def one_tile(tile, carry):
        lanes = pl.ds(pl.multiple_of(tile * width, width), width)
        slot, within = place_of_tile(tile, width)
        q_t = qkv[slot, pair, Q_ROWS, within]
        parts = [slice(first, first + step) for first in range(0, length, step)]
        scores = [biased_scores(keys.at[part], q_t, bias, lanes) for part in parts]
        top = jnp.max(scores[0], axis=0, keepdims=True)
        for more in scores[1:]:
            top = jnp.maximum(top, jnp.max(more, axis=0, keepdims=True))
        total, got = 0.0, 0.0
        for i, part in enumerate(parts):
            held = scores[0] if len(parts) == 1 else biased_scores(keys.at[part], q_t, bias, lanes)
            weight = jnp.exp(held - top)
            total = total + jnp.sum(weight, axis=0, keepdims=True)
            got = got + mm(v_t[:, part], weight.astype(bf16))
        mass[pair, :, lanes] = top + jnp.log(total)
        got = got * (1.0 / total)
        raw[pair, :, lanes] = got
        small_out[slot * pairs + pair, :, within] = got.astype(bf16)
        return carry

    lax.fori_loop(0, length // width, one_tile, 0)


def attend_pair_back(pair, qkv, grad, bias, raw, mass, keys, k_t, v_t, dk, dv, out):
    length = v_t.shape[1]
    pairs = qkv.shape[1]
    width = tile_width(length)
    step = length if length <= 1024 else 512
    gather_rows(qkv, pair, K_ROWS, k_t)
    gather_rows(qkv, pair, V_ROWS, v_t)
    keys[:, :HEAD_DIM] = k_t[...].T
    values = v_t[...].T
    dk[...] = jnp.zeros_like(dk)
    dv[...] = jnp.zeros_like(dv)

    def one_tile(tile, carry):
        lanes = pl.ds(pl.multiple_of(tile * width, width), width)
        slot, within = place_of_tile(tile, width)
        q_t = qkv[slot, pair, Q_ROWS, within]
        g_t = grad[slot, pair, :, within]
        row_dot = jnp.sum(g_t.astype(f32) * raw[pair, :, lanes], axis=0, keepdims=True)
        dq = jnp.zeros(q_t.shape, f32)
        for first in range(0, length, step):
            part = slice(first, first + step)
            probs = jnp.exp(biased_scores(keys.at[part], q_t, bias, lanes) - mass[pair, :, lanes])
            score_grad = (probs * (mm(values[part], g_t) - row_dot)).astype(bf16)
            dq = dq + mm(k_t[:, part], score_grad)
            dk[:, part] += mm_nt(q_t, score_grad)
            dv[:, part] += mm_nt(g_t, probs.astype(bf16))
        out[slot * pairs + pair, Q_ROWS, within] = (dq * score_scale).astype(bf16)
        return carry

    lax.fori_loop(0, length // width, one_tile, 0)
    dk_t, dv_t = dk[...].astype(bf16), dv[...].astype(bf16)
    for slot in range(qkv.shape[0]):
        lanes = slice(slot * 256, (slot + 1) * 256)
        out[slot * pairs + pair, K_ROWS, :] = dk_t[:, lanes]
        out[slot * pairs + pair, V_ROWS, :] = dv_t[:, lanes]


def project_qkv(half, xs, gain, shift, weights, biases, out, n1_t, wait):
    tokens = xs.shape[0] // 2
    here = slice(half * tokens, (half + 1) * tokens)
    vhat, _ = normalise(xs[here, :].astype(f32))
    n1 = (vhat * row(gain) + row(shift)).astype(bf16)
    n1_t[:, here] = n1.T
    for part in range(3):
        wait(part)
        y = mm(n1, weights[part])
        if biases[part] is not None:
            y = y + row(biases[part])
        y = y.astype(bf16)
        if part == 0:
            y = y * jnp.asarray(score_scale, bf16)
        y_t = y.T
        for h in range(HEADS):
            out[h, part * HEAD_DIM : (part + 1) * HEAD_DIM, here] = y_t[
                h * HEAD_DIM : (h + 1) * HEAD_DIM, :
            ]


def fill_bias(place, picks, bias, blocks):
    rows, length = bias.shape
    bias[...] = jnp.zeros_like(bias)

    def one_group(group, carry):
        lanes = pl.ds(pl.multiple_of(group * 128, 128), 128)
        key = lax.broadcasted_iota(jnp.int32, (blocks, 128), 0)
        query = block_at(place, group * 128, (blocks, 128), 1)
        count = (
            jnp.where((key == query - 1) & (query > 0), 1.0, 0.0)
            + jnp.where(key == query, 1.0, 0.0)
            + jnp.where((key == query + 1) & (query < blocks - 1), 1.0, 0.0)
            + jnp.where(key == 0, 1.0, 0.0)
            + jnp.where(key == blocks - 1, 1.0, 0.0)
        )
        half = lax.rem(group, 2)
        window = place.window + half - 2 * half * place.window
        first = (window * place.size + group // 2) * 2
        for side in range(2):
            for r in range(RAND):
                pick = picks[place.window, first + side, r]
                count = count + jnp.where((key == pick) & (query == first + side), 1.0, 0.0)
        listed = count > 0.0
        rest = jnp.where(listed, jnp.log(jnp.maximum(count, 1.0)), masked_score)
        for term in range(3):
            part = rest.astype(bf16)
            bias[term * blocks : (term + 1) * blocks, lanes] = part
            rest = jnp.where(listed, rest - part.astype(f32), 0.0)
        return carry

    lax.fori_loop(0, length // 128, one_group, 0)


def input_back(xs, gain, grad_in, hg, weights, rhs, vec):
    pairs = grad_in.shape[1]
    vhat, rstd = normalise(xs[...].astype(f32))
    err = jnp.zeros(vhat.shape, f32)
    slots = [divmod(h, pairs) for h in range(HEADS)]
    for part in range(3):
        rows = slice(part * HEAD_DIM, (part + 1) * HEAD_DIM)
        rhs[part] = jnp.concatenate([grad_in[s, p, rows, :] for s, p in slots], axis=0).T
        grad = rhs[part]
        err = err + mm_nt(grad, weights[part])
        if part != 1:
            r = 2 + part // 2
            vec[r : r + 1, :] = jnp.sum(grad.astype(f32), axis=0, keepdims=True)
    dv, dgain, dshift = norm_back(err, vhat, rstd, row(gain))
    vec[0:1, :] = dgain
    vec[1:2, :] = dshift
    return (hg[...] + dv).astype(bf16)


def reduce_piece(place, order, out, out_hbm, store, mine, other, bufs, rl, send, recv, free):
    index, col = mine
    cols = pl.ds(col, HALF)
    buf = out.at[index]
    ways = {
        "a": (place.bits["a"], place.across("a")),
        "b": (place.bits["b"], place.across("b")),
        "l": (lax.rem(place.z, 2), place.step_z(1)),
        "h": (place.z // 2, place.step_z(2)),
    }
    hops = [ways[axis] for axis in order]

    def at(start, size):
        return buf.at[span(start, size), cols]

    start, size = 0, D
    spans = []
    for i, (bit, partner) in enumerate(hops):
        size = size // 2
        keep, away = start + bit * size, start + (1 - bit) * size
        if i:
            source = bufs[i - 1]
            at(away, size)[...] = at(away, size)[...] + source[span((1 - bit) * size, size)]
        cp = rcopy(at(away, size), bufs[i], send.at[i], recv.at[i], partner)
        cp.start()
        if i:
            at(keep, size)[...] = at(keep, size)[...] + source[span(bit * size, size)]
        start = keep
        spans.append((keep, size))
        yield
        cp.wait()
        pl.semaphore_signal(free.at[i], inc=1, device_id=partner, device_id_type=MESH)
    held = at(start, size)
    held[...] = held[...] + bufs[-1][...]
    for i in range(place.layer_steps):
        cp = rcopy(held, rl.at[i], send.at[9 + i], recv.at[9 + i], place.layer_swap(i))
        cp.start()
        cp.wait()
        held[...] = held[...] + rl[i]
    for i in reversed(range(len(hops))):
        pl.semaphore_wait(free.at[i], 1)
        held = at(*spans[i])
        cp = rcopy(held, held, send.at[4 + i], recv.at[4 + i], hops[i][1])
        cp.start()
        yield
        cp.wait()
    place.core_open()
    held = buf.at[:, cols]
    cp = rcopy(held, held, send.at[8], recv.at[8], place.core())
    cp.start()
    yield
    cp.wait()
    copies = []
    for i, (block, column) in enumerate((mine, other)):
        where = (block, slice(None), pl.ds(column, HALF))
        copies.append(pltpu.make_async_copy(out.at[where], out_hbm.at[where], store.at[i]))
        copies[-1].start()
    yield
    for copy in copies:
        copy.wait()


def reduce_vectors(place, out, run, got, send, recv):
    for step, device in enumerate((place.core(), place.across("a"), place.across("b"))):
        cp = rcopy(run.at[step], got.at[step], send.at[step], recv.at[step], device)
        cp.start()
        yield
        cp.wait()
        run[step + 1] = run[step] + got[step]
    got[3 + place.z] = run[3]
    cps = [
        rcopy(run.at[3], got.at[3 + place.z], send.at[2 + k], recv.at[6 - k], place.along(k))
        for k in (1, 2, 3)
    ]
    for cp in cps:
        cp.start()
    yield
    for cp in cps:
        cp.wait_send()
    for k in (1, 2, 3):
        slot = got.at[3 + lax.rem(place.z + k, 4)]
        rcopy(slot, slot, send.at[2 + k], recv.at[2 + k], place.along(k)).wait_recv()
    total = got[3]
    for k in range(1, 4):
        total = total + got[3 + k]
    for i in range(place.layer_steps):
        run[4] = total
        cp = rcopy(run.at[4], got.at[7 + i], send.at[6 + i], recv.at[6 + i], place.layer_swap(i))
        cp.start()
        cp.wait()
        total = total + got[7 + i]
    out[...] = total


def layer_kernel(
    dims,
    ids, x, gain1, shift1, bq, bv, bo, gain2, shift2, bup, bdown,
    picks_hbm, cot_hbm, wq_hbm, wk_hbm, wv_hbm, wo_hbm, wup_hbm, wdown_hbm,
    y, dx, vec_out, out_hbm,
    picks, out, xs, y_sent, y_got, wqkv, wo, og, lhs, rhs, n2_t, act_t, pg, hg, dact, up_bias,
    s_og, s_n2, s_act, s_pg, s_lhs, s_rhs,
    head_out, by_head, small_out, att_in, do_in, dqkv_in, bias, raw, mass, keys, k_t, v_t, counts,
    r0, r1, r2, r3, rl, run, got,
    load, store, piece_send, piece_recv, free, core_free, core_send, core_recv,
    qkv_send, qkv_recv, att_send, att_recv, do_send, do_recv, dqkv_send, dqkv_recv,
    count_send, count_recv, vec_send, vec_recv, swap_send, swap_recv,
):
    wins, seqs, windows, pairs = dims
    place = Place(wins, seqs)
    c = place.c
    tokens = x.shape[0] // windows
    kept = pl.ds(pl.multiple_of(place.window * tokens, tokens), tokens)
    moved = pl.ds(pl.multiple_of((1 - place.window) * tokens, tokens), tokens)
    lower, upper = slice(0, tokens), slice(tokens, 2 * tokens)
    length = v_t.shape[1]
    blocks = length // BLOCK
    theirs, ours = 2 * (1 - c), 2 * c

    def up_tile(t):
        return out.at[(t // 2) * 4 + theirs + lax.rem(t, 2)]

    def down_tile(t):
        return out.at[8 + t]

    moves = [(wq_hbm, wqkv.at[0]), (wk_hbm, wqkv.at[1]), (wv_hbm, wqkv.at[2])]
    moves += [(cot_hbm.at[kept], og.at[lower])]
    moves += [(wdown_hbm.at[t * D : (t + 1) * D], down_tile(t)) for t in range(TILES)]
    moves += [(wo_hbm, wo), (picks_hbm, picks)]
    moves += [(wup_hbm.at[:, t * D : (t + 1) * D], up_tile(t)) for t in range(TILES)]
    loads = [pltpu.make_async_copy(src, dst, load.at[i]) for i, (src, dst) in enumerate(moves)]
    for copy in loads:
        copy.start()
    place.greet()

    def swap(i, src, dst):
        copy = rcopy(src, dst, swap_send.at[i], swap_recv.at[i], place.partner())
        copy.start()
        return copy

    x_swap = swap(0, x.at[moved], xs.at[upper])
    lane = lax.broadcasted_iota(jnp.int32, (8, 128), 1)
    member = [jnp.where(lane == ids[w], 1.0, 0.0) for w in range(windows)]
    counts[place.w] = sum(member[1:], member[0])
    mine = counts.at[place.w]
    count_moves = [
        rcopy(mine, mine, count_send.at[k], count_recv.at[k], place.win_at(k))
        for k in range(1, wins)
    ]
    for copy in count_moves:
        copy.start()
    for t in range(TILES):
        up_bias[t : t + 1, :] = bup[t * D : (t + 1) * D].reshape(1, D)
    for p in range(HEADS, head_out.shape[0]):
        head_out[p] = jnp.zeros(head_out.shape[1:], bf16)

    qkv_moves = Exchange(place, pairs, head_out, by_head, qkv_send, qkv_recv)
    att_moves = Exchange(place, pairs, small_out, att_in, att_send, att_recv)
    do_moves = Exchange(place, pairs, small_out, do_in, do_send, do_recv)
    dqkv_moves = Exchange(place, pairs, head_out, dqkv_in, dqkv_send, dqkv_recv)
    halves = (lower, upper)
    xs[lower, :] = x[kept, :]
    for half in range(2):
        if half:
            x_swap.wait()
            cot_swap = swap(1, cot_hbm.at[moved], og.at[upper])
        project_qkv(
            half, xs, gain1, shift1, wqkv, (bq, None, bv), head_out, lhs.at[0],
            (lambda part: None) if half else (lambda part: loads[part].wait()),
        )
        for pair in range(pairs):
            qkv_moves.start(pair, half, halves[half])

    core_moves = {}

    def to_core(name, src, dst):
        i = len(core_moves)
        core_moves[name] = rcopy(src, dst, core_send.at[i], core_recv.at[i], place.core())
        core_moves[name].start()

    waited = set()

    def from_core(*names):
        for name in names:
            if name not in waited:
                waited.add(name)
                core_moves[name].wait()

    to_core("n1", lhs.at[0], s_lhs.at[0])
    block_ones(place, keys, blocks)
    loads[5 + TILES].wait()
    fill_bias(place, picks, bias, blocks)

    for pair in range(pairs):
        for half in range(2):
            qkv_moves.arrived(pair, half, halves[half])
        attend_pair(pair, by_head, bias, keys, k_t, v_t, small_out, raw, mass)
        att_moves.start(pair)
    for copy in count_moves:
        copy.wait_send()
    for k in range(1, wins):
        slot = counts.at[lax.rem(place.w + wins - k, wins)]
        rcopy(slot, slot, count_send.at[k], count_recv.at[k], place.win_at(k)).wait_recv()
    sizes = counts[0]
    for k in range(1, wins):
        sizes = sizes + counts[k]
    first_row = lax.broadcasted_iota(jnp.int32, (8, 128), 0) == 0
    loads[3].wait()
    cot_swap.wait()
    own_size = jnp.sum(
        jnp.where(first_row & (lane == ids[place.window]), sizes, 0.0), keepdims=True
    )
    og[...] = (og[...].astype(f32) * (windows * wins / (GROUPS * own_size))).astype(bf16)
    to_core("og", og, s_og)
    out_grad = og[...]
    for t in range(TILES):
        loads[4 + t].wait()
    early = dact.shape[0] > 1
    if early:
        for t in range(TILES):
            dact[t] = mm_nt(out_grad, down_tile(t)[...])

    for pair in range(pairs):
        att_moves.arrived(pair)
    for h in range(HEADS):
        slot, pair = divmod(h, pairs)
        lhs[1, h * HEAD_DIM : (h + 1) * HEAD_DIM, :] = att_in[slot, pair]
    to_core("att", lhs.at[1], s_lhs.at[1])
    for copy in [loads[4 + TILES]] + loads[6 + TILES :]:
        copy.wait()


    def fill(index, cols, parts):
        @pl.loop(0, D // 256)
        def _(i):
            rows = span(i * 256, 256)
            (left, right), (left2, right2) = parts
            total = mm(left[rows, :], right) + mm(left2[rows, :], right2)
            out[index, rows, cols] = total.astype(bf16)

    def stream(p):
        if p < 8:
            i, h = (p % 4) // 2, p % 2
            index, other = (p // 4) * 4 + ours + i, (p // 4) * 4 + theirs + i
            col = other_col = h * HALF
            cols = slice(col, col + HALF)
            if p < 4:
                from_core("og", ("act", i))
                parts = ((act_t.at[ours + i], og[:, cols]), (s_act.at[i], s_og[:, cols]))
            else:
                from_core("n2", ("pg", i))
                parts = ((n2_t, pg[ours + i, :, cols]), (s_n2, s_pg[i, :, cols]))
        else:
            i = (3, 0, 1, 2)[p - 8]
            index = other = 8 + i
            col = pl.multiple_of(c * HALF, HALF)
            other_col = pl.multiple_of((1 - c) * HALF, HALF)
            cols = pl.ds(col, HALF)
            side = i // 3
            from_core(("n1", "att")[side], ("rhs", i))
            parts = ((lhs.at[side], rhs[i, :, cols]), (s_lhs.at[side], s_rhs[i]))
        fill(index, cols, parts)
        return reduce_piece(
            place, ORDERS[p], out, out_hbm, store.at[p],
            (index, col), (other, other_col),
            [ref.at[p] for ref in (r0, r1, r2, r3)],
            *(ref.at[p] for ref in (rl, piece_send, piece_recv, free)),
        )

    streams = {}
    ended = set()

    def go(p):
        if p not in streams:
            if p == VECTORS:
                streams[p] = reduce_vectors(place, vec_out, run, got, vec_send, vec_recv)
            else:
                streams[p] = stream(p)
        if p not in ended and next(streams[p], True) is not None:
            ended.add(p)


    hidden = xs[...].astype(f32) + (mm(lhs[1].T, wo[...]) + row(bo))
    vhat, rstd = normalise(hidden)
    n2 = (vhat * row(gain2) + row(shift2)).astype(bf16)
    n2_t[...] = n2.T
    to_core("n2", n2_t, s_n2)
    vec = run.at[0]
    vec[...] = jnp.zeros_like(vec)
    total = jnp.zeros(hidden.shape, f32)
    err = jnp.zeros(hidden.shape, f32)
    for i in range(TILES):
        t = (theirs if i < 2 else ours) + i % 2
        up_part, down_part = up_tile(t)[...], down_tile(t)[...]
        pre = mm(n2, up_part) + up_bias[pl.ds(t, 1), :]
        phi = 0.5 * (1.0 + lax.erf(pre * (0.5**0.5)))
        act = (pre * phi).astype(bf16)
        act_t[t] = act.T
        slope = phi + pre * (jnp.exp(-0.5 * pre * pre) * (1.0 / math.sqrt(2.0 * math.pi)))
        back = dact[t] if early else mm_nt(out_grad, down_part)
        grad = (back * slope).astype(bf16)
        pg[t] = grad
        if i < 2:
            to_core(("act", i), act_t.at[t], s_act.at[i])
            to_core(("pg", i), pg.at[t], s_pg.at[i])
        total = total + mm(act, down_part)
        err = err + mm_nt(grad, up_part)
        vec[pl.ds(8 + t, 1), :] = jnp.sum(grad.astype(f32), axis=0, keepdims=True)
        if i == 2:
            go(0)
            go(1)
    pl.semaphore_signal(core_free, inc=1, device_id=place.core(), device_id_type=MESH)
    place.core_free = core_free
    dv, dgain, dshift = norm_back(err, vhat, rstd, row(gain2))
    hidden_grad = out_grad.astype(f32) + dv
    branch = hidden_grad.astype(bf16)
    rhs[3] = branch
    datt_t = mm_nt(branch, wo[...]).astype(bf16).T
    for pair in range(pairs):
        att_moves.sent(pair)
    small_out[:HEADS] = datt_t.reshape(HEADS, HEAD_DIM, 2 * tokens)
    for pair in range(pairs):
        do_moves.start(pair)
    their_cols = pl.ds(pl.multiple_of((1 - c) * HALF, HALF), HALF)
    to_core(("rhs", 3), rhs.at[3, :, their_cols], s_rhs.at[3])
    hg[...] = hidden_grad
    result = (hidden + total + row(bdown)).astype(bf16)
    y[kept, :] = result[:tokens]
    y_sent[0] = result[tokens:]
    y_swap = swap(2, y_sent.at[0], y_got.at[0])
    vec[4:5, :] = jnp.sum(branch.astype(f32), axis=0, keepdims=True)
    vec[5:6, :] = dgain
    vec[6:7, :] = dshift
    vec[7:8, :] = jnp.sum(out_grad.astype(f32), axis=0, keepdims=True)
    for pair in range(pairs):
        for half in range(2):
            qkv_moves.sent(pair, half, halves[half])


    done_pairs = [0]

    def attention():
        pair = done_pairs[0]
        if pair == pairs:
            return
        done_pairs[0] += 1
        do_moves.arrived(pair)

        def scoped(dk, dv):
            attend_pair_back(
                pair, by_head, do_in, bias, raw, mass, keys, k_t, v_t, dk, dv, head_out
            )

        summed = pltpu.VMEM((HEAD_DIM, length), f32)
        pl.run_scoped(scoped, summed, summed)
        dqkv_moves.start(pair)

    def inputs():
        while done_pairs[0] < pairs:
            attention()
        for pair in range(pairs):
            dqkv_moves.arrived(pair)
        result = input_back(xs, gain1, dqkv_in, hg, wqkv, rhs, vec)
        for i in range(3):
            to_core(("rhs", i), rhs.at[i, :, their_cols], s_rhs.at[i])
        dx[kept, :] = result[:tokens]
        y_sent[1] = result[tokens:]
        swaps.append(swap(3, y_sent.at[1], y_got.at[1]))

    swaps = [y_swap]
    actions = {
        "A": attention,
        "W": inputs,
        "X": lambda: from_core(("rhs", 0), ("rhs", 1), ("rhs", 2)),
        "v": functools.partial(go, VECTORS),
    }
    for token in "".join(SCHEDULE):
        if token in actions:
            actions[token]()
        else:
            go(int(token, 16))
    everything = list(range(2 * OWN)) + [VECTORS]
    while len(ended) < len(everything):
        for p in everything:
            go(p)
    from_core(*core_moves)
    for copy in swaps:
        copy.wait()
    y[moved, :] = y_got[0]
    dx[moved, :] = y_got[1]
    for pair in range(pairs):
        do_moves.sent(pair)
        dqkv_moves.sent(pair)


def widen_kernel(
    sums, vec, y, dx, down, up, wq, wk, wv, wo, y_out, dx_out, *rest
):
    low, high, load, store = rest[-4:]
    half = D // 2
    loads = []
    for i in range(4 * OWN):
        rows = slice((i % 2) * half, (i % 2 + 1) * half)
        loads.append(pltpu.make_async_copy(sums.at[i // 2, rows], low.at[i], load.at[i]))
        loads[-1].start()
    y_out[...] = y[...].reshape(y_out.shape)
    dx_out[...] = dx[...].reshape(dx_out.shape)
    for r in range(8):
        rest[r][...] = vec[r, :]
    for r in range(TILES):
        rest[8][r * D : (r + 1) * D] = vec[8 + r, :]
    stores = []
    for i, copy in enumerate(loads):
        block, part = divmod(i, 2)
        rows = slice(part * half, (part + 1) * half)
        if block < 4:
            target = down.at[slice(block * D + part * half, block * D + (part + 1) * half)]
        elif block < 8:
            target = up.at[rows, slice((block - 4) * D, (block - 3) * D)]
        else:
            target = (wq, wk, wv, wo)[block - 8].at[rows]
        copy.wait()
        high[i] = low[i].astype(f32)
        stores.append(pltpu.make_async_copy(high.at[i], target, store.at[i]))
        stores[-1].start()
    for copy in stores:
        copy.wait()


def widen(sums, vec, y, dx, shape):
    struct = jax.ShapeDtypeStruct
    square = struct((D, D), f32)
    vectors = [struct((D,), f32)] * 8 + [struct((FF,), f32)]
    chunks = 4 * OWN
    return pl.pallas_call(
        widen_kernel,
        out_shape=[struct((FF, D), f32), struct((D, FF), f32)]
        + [square] * 4
        + [struct(shape, bf16)] * 2
        + vectors,
        in_specs=[anywhere, in_vmem, in_vmem, in_vmem],
        out_specs=[anywhere] * 6 + [in_vmem] * 11,
        scratch_shapes=[
            pltpu.VMEM((chunks, D // 2, D), bf16),
            pltpu.VMEM((chunks, D // 2, D), f32),
            pltpu.SemaphoreType.DMA((chunks,)),
            pltpu.SemaphoreType.DMA((chunks,)),
        ],
        compiler_params=pltpu.CompilerParams(vmem_limit_bytes=VMEM_LIMIT),
    )(sums, vec, y, dx)


def body(
    tokens,
    cotangent,
    group_ids,
    random_blocks,
    norm1_gain,
    norm1_bias,
    query_weight,
    query_bias,
    key_weight,
    value_weight,
    value_bias,
    out_weight,
    out_bias,
    norm2_gain,
    norm2_bias,
    up_weight,
    up_bias,
    down_weight,
    down_bias,
):
    seqs, wins = lax.axis_size("seq"), lax.axis_size("win")
    windows, here, _ = tokens.shape
    length = here * seqs
    blocks = length // BLOCK
    rows = windows * here
    group = seqs // 2
    pairs = -(-HEADS // group)
    slots = pairs * group
    layer_steps = (seqs // 8).bit_length() - 1
    extra = -(-(HEAD_DIM + 3 * blocks) // 128) * 128 - HEAD_DIM
    dims = (wins, seqs, windows, pairs)
    struct = jax.ShapeDtypeStruct
    dma = pltpu.SemaphoreType.DMA
    vmem = pltpu.VMEM

    x = tokens.reshape(rows, D)
    layer_slots = max(layer_steps, 1)
    pieces = 2 * OWN
    early = TILES if length <= 2048 else 1
    y, dx, vec_sums, sums = pl.pallas_call(
        functools.partial(layer_kernel, dims),
        out_shape=(
            struct((rows, D), bf16),
            struct((rows, D), bf16),
            struct((VEC_ROWS, D), f32),
            struct((pieces, D, D), bf16),
        ),
        in_specs=[in_smem] + [in_vmem] * 10 + [anywhere] * 8,
        out_specs=(in_vmem, in_vmem, in_vmem, anywhere),
        scratch_shapes=[
            pltpu.SMEM(random_blocks.shape, jnp.int32),
            vmem((pieces, D, D), bf16),
            vmem((rows, D), bf16),
            vmem((2, here, D), bf16),
            vmem((2, here, D), bf16),
            vmem((3, D, D), bf16),
            vmem((D, D), bf16),
            vmem((rows, D), bf16),
            vmem((2, D, rows), bf16),
            vmem((4, rows, D), bf16),
            vmem((D, rows), bf16),
            vmem((TILES, D, rows), bf16),
            vmem((TILES, rows, D), bf16),
            vmem((rows, D), f32),
            vmem((early, rows, D) if early > 1 else (1, 8, 128), f32),
            vmem((8, D), f32),
            vmem((rows, D), bf16),
            vmem((D, rows), bf16),
            vmem((2, D, rows), bf16),
            vmem((2, rows, D), bf16),
            vmem((2, D, rows), bf16),
            vmem((4, rows, HALF), bf16),
            vmem((slots, 3 * HEAD_DIM, rows), bf16),
            vmem((group, pairs, 3 * HEAD_DIM, rows), bf16),
            vmem((slots, HEAD_DIM, rows), bf16),
            vmem((group, pairs, HEAD_DIM, rows), bf16),
            vmem((group, pairs, HEAD_DIM, rows), bf16),
            vmem((group, pairs, 3 * HEAD_DIM, rows), bf16),
            vmem((extra, length), bf16),
            vmem((pairs, HEAD_DIM, length), f32),
            vmem((pairs, 1, length), f32),
            vmem((length, HEAD_DIM + extra), bf16),
            vmem((HEAD_DIM, length), bf16),
            vmem((HEAD_DIM, length), bf16),
            vmem((wins, 8, 128), f32),
            vmem((pieces, D // 2, HALF), bf16),
            vmem((pieces, D // 4, HALF), bf16),
            vmem((pieces, D // 8, HALF), bf16),
            vmem((pieces, D // 16, HALF), bf16),
            vmem((pieces, layer_slots, D // 16, HALF), bf16),
            vmem((5, VEC_ROWS, D), f32),
            vmem((7 + layer_slots, VEC_ROWS, D), f32),
            dma((6 + 2 * TILES,)),
            dma((pieces, 2)),
            dma((pieces, 9 + layer_slots)),
            dma((pieces, 9 + layer_slots)),
            pltpu.SemaphoreType.REGULAR((pieces, 4)),
            pltpu.SemaphoreType.REGULAR,
            dma((12,)),
            dma((12,)),
        ]
        + [dma((group, pairs, 2))] * 8
        + [dma((wins,))] * 2
        + [dma((6 + layer_slots,))] * 2
        + [dma((4,))] * 2,
        compiler_params=pltpu.CompilerParams(
            collective_id=0, has_side_effects=True, vmem_limit_bytes=VMEM_LIMIT
        ),
    )(
        group_ids, x, norm1_gain, norm1_bias, query_bias, value_bias, out_bias,
        norm2_gain, norm2_bias, up_bias, down_bias, random_blocks, cotangent.reshape(rows, D), query_weight,
        key_weight, value_weight, out_weight, up_weight, down_weight,
    )

    (
        down_grad, up_grad, query_grad, key_grad, value_grad, out_grad, output, input_grad,
        gain1_grad, shift1_grad, query_bias_grad, value_bias_grad, out_bias_grad,
        gain2_grad, shift2_grad, down_bias_grad, up_bias_grad,
    ) = widen(sums, vec_sums, y, dx, tokens.shape)
    return (
        output, input_grad, gain1_grad, shift1_grad, query_grad, query_bias_grad, key_grad,
        value_grad, value_bias_grad, out_grad, out_bias_grad, gain2_grad, shift2_grad, up_grad,
        up_bias_grad, down_grad, down_bias_grad,
    )


def solution(mesh):
    split = P("win", "seq", None)
    return jax.shard_map(
        body,
        mesh=mesh,
        in_specs=(split, split, P("win"), P("win", None, None)) + (P(),) * 15,
        out_specs=(split, split) + (P(),) * 15,
        check_vma=False,
    )
```

```python
import functools
import math

import jax
import jax.numpy as jnp
from jax import lax
from jax.experimental import pallas as pl
from jax.experimental.pallas import tpu as pltpu
from jax.sharding import PartitionSpec as P

D = 768
HEADS = 12
HEAD_DIM = 64
FF = 3072
BLOCK = 64
RAND = 3
GROUPS = 8
TILES = FF // D
VEC_ROWS = 16
OWN = 6
HALF = D // 2
VECTORS = 12
ORDERS = (
    "labh", "balh", "ablh", "balh",
    "ablh", "balh", "ablh", "balh",
    "ablh", "balh", "ablh", "balh",
)
SCHEDULE = (
    "2014AAA25403216057Wv36124v0X875v936b8v1a",
    "932v67405vb71a3v82109684a2b59713426a08b5",
    "97132641a526308b90754a8b594a36b8376a9b77",
    "8989abab",
)

MESH = pl.DeviceIdType.MESH
VMEM_LIMIT = 63 << 20
epsilon = 1e-05
masked_score = -1e30
score_scale = HEAD_DIM ** (-0.5)
f32 = jnp.float32
bf16 = jnp.bfloat16

in_vmem = pl.BlockSpec(memory_space=pltpu.VMEM)
in_smem = pl.BlockSpec(memory_space=pltpu.SMEM)
anywhere = pl.BlockSpec(memory_space=pl.ANY)


def mm(left, right):
    return jnp.dot(left, right, preferred_element_type=f32)


def mm_nt(left, right):
    return lax.dot_general(left, right, (((1,), (1,)), ((), ())), preferred_element_type=f32)


def row(ref):
    return ref[...].reshape(1, -1)


def normalise(v):
    centre = v - jnp.mean(v, axis=-1, keepdims=True)
    rstd = lax.rsqrt(jnp.mean(centre * centre, axis=-1, keepdims=True) + epsilon)
    return centre * rstd, rstd


def norm_back(err, vhat, rstd, gain):
    g = err * gain
    dv = rstd * (
        g - jnp.mean(g, axis=-1, keepdims=True) - vhat * jnp.mean(g * vhat, axis=-1, keepdims=True)
    )
    return dv, jnp.sum(err * vhat, axis=0, keepdims=True), jnp.sum(err, axis=0, keepdims=True)


def rcopy(src, dst, send, recv, device):
    return pltpu.make_async_remote_copy(
        src, dst, send, recv, device_id=device, device_id_type=MESH
    )


def span(start, size):
    return pl.ds(pl.multiple_of(start, 16), size)


class Place:
    def __init__(self, wins, seqs):
        self.wins, self.seqs = wins, seqs
        self.layers = seqs // 8
        self.w = lax.axis_index("win")
        self.s = lax.axis_index("seq")
        self.c = lax.rem(self.s, 2)
        self.z = lax.rem(self.s // 2, 4)
        self.layer = self.s // 8
        self.layer_steps = (seqs // 8).bit_length() - 1
        self.size = seqs // 2
        self.window = self.s // self.size
        self.g = lax.rem(self.s, self.size)
        self.base = self.s - self.g
        self.core_free = None
        self.bits = {"a": lax.rem(self.w, 2), "b": self.w // 2}

    def core(self):
        return (self.w, self.s + 1 - 2 * self.c)

    def across(self, axis):
        step = 1 if axis == "a" else 2
        return (self.w + step - 2 * step * self.bits[axis], self.s)

    def along(self, k):
        return (self.w, self.layer * 8 + lax.rem(self.z + k, 4) * 2 + self.c)

    def layer_swap(self, i):
        step = 2**i
        bit = lax.rem(self.layer // step, 2)
        return (self.w, self.s + 8 * step * (1 - 2 * bit))

    def step_z(self, step):
        bit = lax.rem(self.z // step, 2)
        return (self.w, self.s + 2 * step * (1 - 2 * bit))

    def core_open(self):
        if self.core_free is not None:
            pl.semaphore_wait(self.core_free, 1)
            self.core_free = None

    def group_at(self, k):
        return (self.w, self.base + lax.rem(self.g + k, self.size))

    def partner(self):
        return (self.w, lax.rem(self.s + self.size, self.seqs))

    def win_at(self, k):
        return (lax.rem(self.w + k, self.wins), self.s)

    def greet(self):
        barrier = pltpu.get_barrier_semaphore()

        def one(k, carry):
            pl.semaphore_signal(barrier, inc=1, device_id=self.group_at(k), device_id_type=MESH)
            return carry

        lax.fori_loop(1, self.size, one, 0)
        others = [self.partner()]
        others += [self.win_at(k) for k in range(1, self.wins)]
        others += [self.layer_swap(i) for i in range(self.layer_steps)]
        for peer in others:
            pl.semaphore_signal(barrier, inc=1, device_id=peer, device_id_type=MESH)
        pl.semaphore_wait(barrier, self.size - 1 + len(others))


class Exchange:
    def __init__(self, place, pairs, out, into, send, recv):
        self.place, self.pairs = place, pairs
        self.out, self.into, self.send, self.recv = out, into, send, recv

    def copy(self, k, pair, part, lanes):
        place = self.place
        target = lax.rem(place.g + k, place.size)
        return rcopy(
            self.out.at[target * self.pairs + pair, :, lanes],
            self.into.at[place.g, pair, :, lanes],
            self.send.at[pair, part],
            self.recv.at[pair, part],
            place.group_at(k),
        )

    def start(self, pair, part=0, lanes=slice(None)):
        def one(k, carry):
            self.copy(k, pair, part, lanes).start()
            return carry

        place = self.place
        lax.fori_loop(1, place.size, one, 0)
        self.into[place.g, pair, :, lanes] = self.out[place.g * self.pairs + pair, :, lanes]

    def whole(self, ref, pair, part, lanes):
        return rcopy(
            ref, ref, self.send.at[pair, part], self.recv.at[pair, part], self.place.group_at(1)
        )

    def arrived(self, pair, part=0, lanes=slice(None)):
        held = self.into.at[pl.ds(0, self.place.size - 1), pair, :, lanes]
        self.whole(held, pair, part, lanes).wait_recv()

    def sent(self, pair, part=0, lanes=slice(None)):
        held = self.out.at[pl.ds(0, self.place.size - 1), :, lanes]
        self.whole(held, pair, part, lanes).wait_send()


Q_ROWS, K_ROWS, V_ROWS = (slice(i * HEAD_DIM, (i + 1) * HEAD_DIM) for i in range(3))


def tile_width(length):
    return 256 if length <= 2048 else 128


def block_at(place, first, shape, axis):
    index = first + lax.broadcasted_iota(jnp.int32, shape, axis)
    slot, half = index // 256, lax.rem(index // 128, 2)
    window = place.window + half - 2 * half * place.window
    return (window * place.size + slot) * 2 + lax.rem(index // BLOCK, 2)


def block_ones(place, keys, blocks):
    length, lanes = keys.shape

    def one_group(group, carry):
        shape = (256, lanes)
        part = lax.broadcasted_iota(jnp.int32, shape, 1) - HEAD_DIM
        block = block_at(place, group * 256, shape, 0)
        hit = (part == block) | (part == block + blocks) | (part == block + 2 * blocks)
        keys[span(group * 256, 256), :] = jnp.where(hit, 1.0, 0.0).astype(bf16)
        return carry

    lax.fori_loop(0, length // 256, one_group, 0)


def gather_rows(ref, pair, rows, into):
    tokens = ref.shape[3]
    for s in range(ref.shape[0]):
        into[: rows.stop - rows.start, s * tokens : (s + 1) * tokens] = ref[s, pair, rows, :]


def place_of_tile(tile, width):
    per_slot = 256 // width
    if per_slot == 1:
        return tile, slice(None)
    return tile // per_slot, pl.ds(pl.multiple_of(lax.rem(tile, per_slot) * width, width), width)


def biased_scores(keys, q_t, bias, lanes):
    return mm(keys[...], jnp.concatenate([q_t, bias[:, lanes]], axis=0))


def attend_pair(pair, qkv, bias, keys, k_t, v_t, small_out, raw, mass):
    length = v_t.shape[1]
    pairs = qkv.shape[1]
    width = tile_width(length)
    step = length if length <= 1024 else 512
    gather_rows(qkv, pair, K_ROWS, k_t)
    gather_rows(qkv, pair, V_ROWS, v_t)
    keys[:, :HEAD_DIM] = k_t[...].T

    def one_tile(tile, carry):
        lanes = pl.ds(pl.multiple_of(tile * width, width), width)
        slot, within = place_of_tile(tile, width)
        q_t = qkv[slot, pair, Q_ROWS, within]
        parts = [slice(first, first + step) for first in range(0, length, step)]
        scores = [biased_scores(keys.at[part], q_t, bias, lanes) for part in parts]
        top = jnp.max(scores[0], axis=0, keepdims=True)
        for more in scores[1:]:
            top = jnp.maximum(top, jnp.max(more, axis=0, keepdims=True))
        total, got = 0.0, 0.0
        for i, part in enumerate(parts):
            held = scores[0] if len(parts) == 1 else biased_scores(keys.at[part], q_t, bias, lanes)
            weight = jnp.exp(held - top)
            total = total + jnp.sum(weight, axis=0, keepdims=True)
            got = got + mm(v_t[:, part], weight.astype(bf16))
        mass[pair, :, lanes] = top + jnp.log(total)
        got = got * (1.0 / total)
        raw[pair, :, lanes] = got
        small_out[slot * pairs + pair, :, within] = got.astype(bf16)
        return carry

    lax.fori_loop(0, length // width, one_tile, 0)


def attend_pair_back(pair, qkv, grad, bias, raw, mass, keys, k_t, v_t, dk, dv, out):
    length = v_t.shape[1]
    pairs = qkv.shape[1]
    width = tile_width(length)
    step = length if length <= 1024 else 512
    gather_rows(qkv, pair, K_ROWS, k_t)
    gather_rows(qkv, pair, V_ROWS, v_t)
    keys[:, :HEAD_DIM] = k_t[...].T
    values = v_t[...].T
    dk[...] = jnp.zeros_like(dk)
    dv[...] = jnp.zeros_like(dv)

    def one_tile(tile, carry):
        lanes = pl.ds(pl.multiple_of(tile * width, width), width)
        slot, within = place_of_tile(tile, width)
        q_t = qkv[slot, pair, Q_ROWS, within]
        g_t = grad[slot, pair, :, within]
        row_dot = jnp.sum(g_t.astype(f32) * raw[pair, :, lanes], axis=0, keepdims=True)
        dq = jnp.zeros(q_t.shape, f32)
        for first in range(0, length, step):
            part = slice(first, first + step)
            probs = jnp.exp(biased_scores(keys.at[part], q_t, bias, lanes) - mass[pair, :, lanes])
            score_grad = (probs * (mm(values[part], g_t) - row_dot)).astype(bf16)
            dq = dq + mm(k_t[:, part], score_grad)
            dk[:, part] += mm_nt(q_t, score_grad)
            dv[:, part] += mm_nt(g_t, probs.astype(bf16))
        out[slot * pairs + pair, Q_ROWS, within] = (dq * score_scale).astype(bf16)
        return carry

    lax.fori_loop(0, length // width, one_tile, 0)
    dk_t, dv_t = dk[...].astype(bf16), dv[...].astype(bf16)
    for slot in range(qkv.shape[0]):
        lanes = slice(slot * 256, (slot + 1) * 256)
        out[slot * pairs + pair, K_ROWS, :] = dk_t[:, lanes]
        out[slot * pairs + pair, V_ROWS, :] = dv_t[:, lanes]


def project_qkv(half, xs, gain, shift, weights, biases, out, n1_t, wait):
    tokens = xs.shape[0] // 2
    here = slice(half * tokens, (half + 1) * tokens)
    vhat, _ = normalise(xs[here, :].astype(f32))
    n1 = (vhat * row(gain) + row(shift)).astype(bf16)
    n1_t[:, here] = n1.T
    for part in range(3):
        wait(part)
        y = mm(n1, weights[part])
        if biases[part] is not None:
            y = y + row(biases[part])
        y = y.astype(bf16)
        if part == 0:
            y = y * jnp.asarray(score_scale, bf16)
        y_t = y.T
        for h in range(HEADS):
            out[h, part * HEAD_DIM : (part + 1) * HEAD_DIM, here] = y_t[
                h * HEAD_DIM : (h + 1) * HEAD_DIM, :
            ]


def fill_bias(place, picks, bias, blocks):
    rows, length = bias.shape
    bias[...] = jnp.zeros_like(bias)

    def one_group(group, carry):
        lanes = pl.ds(pl.multiple_of(group * 128, 128), 128)
        key = lax.broadcasted_iota(jnp.int32, (blocks, 128), 0)
        query = block_at(place, group * 128, (blocks, 128), 1)
        count = (
            jnp.where((key == query - 1) & (query > 0), 1.0, 0.0)
            + jnp.where(key == query, 1.0, 0.0)
            + jnp.where((key == query + 1) & (query < blocks - 1), 1.0, 0.0)
            + jnp.where(key == 0, 1.0, 0.0)
            + jnp.where(key == blocks - 1, 1.0, 0.0)
        )
        half = lax.rem(group, 2)
        window = place.window + half - 2 * half * place.window
        first = (window * place.size + group // 2) * 2
        for side in range(2):
            for r in range(RAND):
                pick = picks[r, place.window, first + side]
                count = count + jnp.where((key == pick) & (query == first + side), 1.0, 0.0)
        listed = count > 0.0
        rest = jnp.where(listed, jnp.log(jnp.maximum(count, 1.0)), masked_score)
        for term in range(3):
            part = rest.astype(bf16)
            bias[term * blocks : (term + 1) * blocks, lanes] = part
            rest = jnp.where(listed, rest - part.astype(f32), 0.0)
        return carry

    lax.fori_loop(0, length // 128, one_group, 0)


def input_back(xs, gain, grad_in, hg, weights, rhs, vec):
    pairs = grad_in.shape[1]
    vhat, rstd = normalise(xs[...].astype(f32))
    err = jnp.zeros(vhat.shape, f32)
    slots = [divmod(h, pairs) for h in range(HEADS)]
    for part in range(3):
        rows = slice(part * HEAD_DIM, (part + 1) * HEAD_DIM)
        rhs[part] = jnp.concatenate([grad_in[s, p, rows, :] for s, p in slots], axis=0).T
        grad = rhs[part]
        err = err + mm_nt(grad, weights[part])
        if part != 1:
            r = 2 + part // 2
            vec[r : r + 1, :] = jnp.sum(grad.astype(f32), axis=0, keepdims=True)
    dv, dgain, dshift = norm_back(err, vhat, rstd, row(gain))
    vec[0:1, :] = dgain
    vec[1:2, :] = dshift
    return (hg[...] + dv).astype(bf16)


def reduce_piece(place, order, out, out_hbm, store, mine, other, bufs, rl, send, recv, free):
    index, col = mine
    cols = pl.ds(col, HALF)
    buf = out.at[index]
    ways = {
        "a": (place.bits["a"], place.across("a")),
        "b": (place.bits["b"], place.across("b")),
        "l": (lax.rem(place.z, 2), place.step_z(1)),
        "h": (place.z // 2, place.step_z(2)),
    }
    hops = [ways[axis] for axis in order]

    def at(start, size):
        return buf.at[span(start, size), cols]

    start, size = 0, D
    spans = []
    for i, (bit, partner) in enumerate(hops):
        size = size // 2
        keep, away = start + bit * size, start + (1 - bit) * size
        if i:
            source = bufs[i - 1]
            at(away, size)[...] = at(away, size)[...] + source[span((1 - bit) * size, size)]
        cp = rcopy(at(away, size), bufs[i], send, recv.at[i], partner)
        cp.start()
        if i:
            at(keep, size)[...] = at(keep, size)[...] + source[span(bit * size, size)]
        start = keep
        spans.append((keep, size))
        yield
        cp.wait()
        pl.semaphore_signal(free, inc=1, device_id=partner, device_id_type=MESH)
    held = at(start, size)
    held[...] = held[...] + bufs[-1][...]
    for i in range(place.layer_steps):
        cp = rcopy(held, rl.at[i], send, recv.at[9 + i], place.layer_swap(i))
        cp.start()
        cp.wait()
        held[...] = held[...] + rl[i]
    pl.semaphore_wait(free, len(hops))
    for i in reversed(range(len(hops))):
        held = at(*spans[i])
        cp = rcopy(held, held, send, recv.at[4 + i], hops[i][1])
        cp.start()
        yield
        cp.wait()
    place.core_open()
    held = buf.at[:, cols]
    cp = rcopy(held, held, send, recv.at[8], place.core())
    cp.start()
    yield
    cp.wait()
    for block, column in (mine, other):
        where = (block, slice(None), pl.ds(column, HALF))
        pltpu.make_async_copy(out.at[where], out_hbm.at[where], store).start()


def reduce_vectors(place, out, run, got, send, recv):
    for step, device in enumerate((place.core(), place.across("a"), place.across("b"))):
        cp = rcopy(run.at[step], got.at[step], send.at[step], recv.at[step], device)
        cp.start()
        yield
        cp.wait()
        run[step + 1] = run[step] + got[step]
    got[3 + place.z] = run[3]
    cps = [
        rcopy(run.at[3], got.at[3 + place.z], send.at[2 + k], recv.at[6 - k], place.along(k))
        for k in (1, 2, 3)
    ]
    for cp in cps:
        cp.start()
    yield
    for cp in cps:
        cp.wait_send()
    for k in (1, 2, 3):
        slot = got.at[3 + lax.rem(place.z + k, 4)]
        rcopy(slot, slot, send.at[2 + k], recv.at[2 + k], place.along(k)).wait_recv()
    total = got[3]
    for k in range(1, 4):
        total = total + got[3 + k]
    for i in range(place.layer_steps):
        run[4] = total
        cp = rcopy(run.at[4], got.at[7 + i], send.at[6 + i], recv.at[6 + i], place.layer_swap(i))
        cp.start()
        cp.wait()
        total = total + got[7 + i]
    out[...] = total


def layer_kernel(
    dims,
    ids, x, gain1, shift1, bq, bv, bo, gain2, shift2, bup, bdown,
    picks_hbm, cot_hbm, wq_hbm, wk_hbm, wv_hbm, wo_hbm, wup_hbm, wdown_hbm,
    y, dx, vec_out, out_hbm,
    picks, out, xs, y_sent, y_got, wqkv, wo, og, lhs, rhs, n2_t, act_t, pg, hg, dact, up_bias,
    s_og, s_n2, s_act, s_pg, s_lhs, s_rhs,
    head_out, by_head, small_out, att_in, do_in, dqkv_in, bias, raw, mass, keys, k_t, v_t, counts,
    r0, r1, r2, r3, rl, run, got,
    load, store, piece_send, piece_recv, free, core_free, core_send, core_recv,
    qkv_send, qkv_recv, att_send, att_recv, do_send, do_recv, dqkv_send, dqkv_recv,
    count_send, count_recv, vec_send, vec_recv, swap_send, swap_recv,
):
    wins, seqs, windows, pairs = dims
    place = Place(wins, seqs)
    c = place.c
    tokens = x.shape[0] // windows
    kept = pl.ds(pl.multiple_of(place.window * tokens, tokens), tokens)
    moved = pl.ds(pl.multiple_of((1 - place.window) * tokens, tokens), tokens)
    lower, upper = slice(0, tokens), slice(tokens, 2 * tokens)
    length = v_t.shape[1]
    blocks = length // BLOCK
    theirs, ours = 2 * (1 - c), 2 * c

    def up_tile(t):
        return out.at[(t // 2) * 4 + theirs + lax.rem(t, 2)]

    def down_tile(t):
        return out.at[8 + t]

    moves = [(wq_hbm, wqkv.at[0]), (wk_hbm, wqkv.at[1]), (wv_hbm, wqkv.at[2])]
    moves += [(cot_hbm.at[kept], og.at[lower])]
    moves += [(wdown_hbm.at[t * D : (t + 1) * D], down_tile(t)) for t in range(TILES)]
    moves += [(wo_hbm, wo), (picks_hbm, picks)]
    moves += [(wup_hbm.at[:, t * D : (t + 1) * D], up_tile(t)) for t in range(TILES)]
    loads = [pltpu.make_async_copy(src, dst, load.at[i]) for i, (src, dst) in enumerate(moves)]
    for copy in loads:
        copy.start()
    place.greet()

    def swap(i, src, dst):
        copy = rcopy(src, dst, swap_send.at[i], swap_recv.at[i], place.partner())
        copy.start()
        return copy

    x_swap = swap(0, x.at[moved], xs.at[upper])
    lane = lax.broadcasted_iota(jnp.int32, (8, 128), 1)
    member = [jnp.where(lane == ids[w], 1.0, 0.0) for w in range(windows)]
    counts[place.w] = sum(member[1:], member[0])
    mine = counts.at[place.w]
    count_moves = [
        rcopy(mine, mine, count_send.at[k], count_recv.at[k], place.win_at(k))
        for k in range(1, wins)
    ]
    for copy in count_moves:
        copy.start()
    for t in range(TILES):
        up_bias[t : t + 1, :] = bup[t * D : (t + 1) * D].reshape(1, D)
    for p in range(HEADS, head_out.shape[0]):
        head_out[p] = jnp.zeros(head_out.shape[1:], bf16)

    qkv_moves = Exchange(place, pairs, head_out, by_head, qkv_send, qkv_recv)
    att_moves = Exchange(place, pairs, small_out, att_in, att_send, att_recv)
    do_moves = Exchange(place, pairs, small_out, do_in, do_send, do_recv)
    dqkv_moves = Exchange(place, pairs, head_out, dqkv_in, dqkv_send, dqkv_recv)
    halves = (lower, upper)
    xs[lower, :] = x[kept, :]
    for half in range(2):
        if half:
            x_swap.wait()
            cot_swap = swap(1, cot_hbm.at[moved], og.at[upper])
        project_qkv(
            half, xs, gain1, shift1, wqkv, (bq, None, bv), head_out, lhs.at[0],
            (lambda part: None) if half else (lambda part: loads[part].wait()),
        )
        for pair in range(pairs):
            qkv_moves.start(pair, half, halves[half])

    core_moves = {}

    def to_core(name, src, dst):
        i = len(core_moves)
        core_moves[name] = rcopy(src, dst, core_send.at[i], core_recv.at[i], place.core())
        core_moves[name].start()

    waited = set()

    def from_core(*names):
        for name in names:
            if name not in waited:
                waited.add(name)
                core_moves[name].wait()

    to_core("n1", lhs.at[0], s_lhs.at[0])
    block_ones(place, keys, blocks)
    loads[5 + TILES].wait()
    fill_bias(place, picks, bias, blocks)

    for pair in range(pairs):
        for half in range(2):
            qkv_moves.arrived(pair, half, halves[half])
        attend_pair(pair, by_head, bias, keys, k_t, v_t, small_out, raw, mass)
        att_moves.start(pair)
    for copy in count_moves:
        copy.wait_send()
    for k in range(1, wins):
        slot = counts.at[lax.rem(place.w + wins - k, wins)]
        rcopy(slot, slot, count_send.at[k], count_recv.at[k], place.win_at(k)).wait_recv()
    sizes = counts[0]
    for k in range(1, wins):
        sizes = sizes + counts[k]
    first_row = lax.broadcasted_iota(jnp.int32, (8, 128), 0) == 0
    loads[3].wait()
    cot_swap.wait()
    own_size = jnp.sum(
        jnp.where(first_row & (lane == ids[place.window]), sizes, 0.0), keepdims=True
    )
    og[...] = (og[...].astype(f32) * (windows * wins / (GROUPS * own_size))).astype(bf16)
    to_core("og", og, s_og)
    out_grad = og[...]
    for t in range(TILES):
        loads[4 + t].wait()
    early = dact.shape[0] > 1
    if early:
        for t in range(TILES):
            dact[t] = mm_nt(out_grad, down_tile(t)[...])

    for pair in range(pairs):
        att_moves.arrived(pair)
    for h in range(HEADS):
        slot, pair = divmod(h, pairs)
        lhs[1, h * HEAD_DIM : (h + 1) * HEAD_DIM, :] = att_in[slot, pair]
    to_core("att", lhs.at[1], s_lhs.at[1])
    for copy in [loads[4 + TILES]] + loads[6 + TILES :]:
        copy.wait()


    def fill(index, cols, parts):
        @pl.loop(0, D // 256)
        def _(i):
            rows = span(i * 256, 256)
            (left, right), (left2, right2) = parts
            total = mm(left[rows, :], right) + mm(left2[rows, :], right2)
            out[index, rows, cols] = total.astype(bf16)

    def stream(p):
        if p < 8:
            i, h = (p % 4) // 2, p % 2
            index, other = (p // 4) * 4 + ours + i, (p // 4) * 4 + theirs + i
            col = other_col = h * HALF
            cols = slice(col, col + HALF)
            if p < 4:
                from_core("og", ("act", i))
                parts = ((act_t.at[ours + i], og[:, cols]), (s_act.at[i], s_og[:, cols]))
            else:
                from_core("n2", ("pg", i))
                parts = ((n2_t, pg[ours + i, :, cols]), (s_n2, s_pg[i, :, cols]))
        else:
            i = (3, 0, 1, 2)[p - 8]
            index = other = 8 + i
            col = pl.multiple_of(c * HALF, HALF)
            other_col = pl.multiple_of((1 - c) * HALF, HALF)
            cols = pl.ds(col, HALF)
            side = i // 3
            from_core(("n1", "att")[side], ("rhs", i))
            parts = ((lhs.at[side], rhs[i, :, cols]), (s_lhs.at[side], s_rhs[i]))
        fill(index, cols, parts)
        return reduce_piece(
            place, ORDERS[p], out, out_hbm, store,
            (index, col), (other, other_col),
            [ref.at[p] for ref in (r0, r1, r2, r3)],
            *(ref.at[p] for ref in (rl, piece_send, piece_recv, free)),
        )

    streams = {}
    ended = set()

    def go(p):
        if p not in streams:
            if p == VECTORS:
                streams[p] = reduce_vectors(place, vec_out, run, got, vec_send, vec_recv)
            else:
                streams[p] = stream(p)
        if p not in ended and next(streams[p], True) is not None:
            ended.add(p)


    hidden = xs[...].astype(f32) + (mm(lhs[1].T, wo[...]) + row(bo))
    vhat, rstd = normalise(hidden)
    n2 = (vhat * row(gain2) + row(shift2)).astype(bf16)
    n2_t[...] = n2.T
    to_core("n2", n2_t, s_n2)
    vec = run.at[0]
    vec[...] = jnp.zeros_like(vec)
    total = jnp.zeros(hidden.shape, f32)
    err = jnp.zeros(hidden.shape, f32)
    for i in range(TILES):
        t = (theirs if i < 2 else ours) + i % 2
        up_part, down_part = up_tile(t)[...], down_tile(t)[...]
        pre = mm(n2, up_part) + up_bias[pl.ds(t, 1), :]
        phi = 0.5 * (1.0 + lax.erf(pre * (0.5**0.5)))
        act = (pre * phi).astype(bf16)
        act_t[t] = act.T
        slope = phi + pre * (jnp.exp(-0.5 * pre * pre) * (1.0 / math.sqrt(2.0 * math.pi)))
        back = dact[t] if early else mm_nt(out_grad, down_part)
        grad = (back * slope).astype(bf16)
        pg[t] = grad
        if i < 2:
            to_core(("act", i), act_t.at[t], s_act.at[i])
            to_core(("pg", i), pg.at[t], s_pg.at[i])
        total = total + mm(act, down_part)
        err = err + mm_nt(grad, up_part)
        vec[pl.ds(8 + t, 1), :] = jnp.sum(grad.astype(f32), axis=0, keepdims=True)
        if i == 2:
            for p in (0, 1, 4, 5):
                go(p)
    pl.semaphore_signal(core_free, inc=1, device_id=place.core(), device_id_type=MESH)
    place.core_free = core_free
    dv, dgain, dshift = norm_back(err, vhat, rstd, row(gain2))
    hidden_grad = out_grad.astype(f32) + dv
    branch = hidden_grad.astype(bf16)
    rhs[3] = branch
    datt_t = mm_nt(branch, wo[...]).astype(bf16).T
    for pair in range(pairs):
        att_moves.sent(pair)
    small_out[:HEADS] = datt_t.reshape(HEADS, HEAD_DIM, 2 * tokens)
    for pair in range(pairs):
        do_moves.start(pair)
    their_cols = pl.ds(pl.multiple_of((1 - c) * HALF, HALF), HALF)
    to_core(("rhs", 3), rhs.at[3, :, their_cols], s_rhs.at[3])
    hg[...] = hidden_grad
    result = (hidden + total + row(bdown)).astype(bf16)
    y[kept, :] = result[:tokens]
    y_sent[0] = result[tokens:]
    y_swap = swap(2, y_sent.at[0], y_got.at[0])
    vec[4:5, :] = jnp.sum(branch.astype(f32), axis=0, keepdims=True)
    vec[5:6, :] = dgain
    vec[6:7, :] = dshift
    vec[7:8, :] = jnp.sum(out_grad.astype(f32), axis=0, keepdims=True)
    for pair in range(pairs):
        for half in range(2):
            qkv_moves.sent(pair, half, halves[half])


    done_pairs = [0]

    def attention():
        pair = done_pairs[0]
        if pair == pairs:
            return
        done_pairs[0] += 1
        do_moves.arrived(pair)

        def scoped(dk, dv):
            attend_pair_back(
                pair, by_head, do_in, bias, raw, mass, keys, k_t, v_t, dk, dv, head_out
            )

        summed = pltpu.VMEM((HEAD_DIM, length), f32)
        pl.run_scoped(scoped, summed, summed)
        dqkv_moves.start(pair)

    def inputs():
        while done_pairs[0] < pairs:
            attention()
        for pair in range(pairs):
            dqkv_moves.arrived(pair)
        result = input_back(xs, gain1, dqkv_in, hg, wqkv, rhs, vec)
        for i in range(3):
            to_core(("rhs", i), rhs.at[i, :, their_cols], s_rhs.at[i])
        dx[kept, :] = result[:tokens]
        y_sent[1] = result[tokens:]
        swaps.append(swap(3, y_sent.at[1], y_got.at[1]))

    swaps = [y_swap]
    actions = {
        "A": attention,
        "W": inputs,
        "X": lambda: from_core(("rhs", 0), ("rhs", 1), ("rhs", 2)),
        "v": functools.partial(go, VECTORS),
    }
    for token in "".join(SCHEDULE):
        if token in actions:
            actions[token]()
        else:
            go(int(token, 16))
    everything = list(range(2 * OWN)) + [VECTORS]
    while len(ended) < len(everything):
        for p in everything:
            go(p)
    pltpu.make_async_copy(out, out_hbm, store).wait()
    from_core(*core_moves)
    for copy in swaps:
        copy.wait()
    y[moved, :] = y_got[0]
    dx[moved, :] = y_got[1]
    for pair in range(pairs):
        do_moves.sent(pair)
        dqkv_moves.sent(pair)


def widen_kernel(
    sums, vec, y, dx, down, up, wq, wk, wv, wo, y_out, dx_out, *rest
):
    low, high, load, store = rest[-4:]
    half = D // 2
    loads = []
    for i in range(4 * OWN):
        rows = slice((i % 2) * half, (i % 2 + 1) * half)
        loads.append(pltpu.make_async_copy(sums.at[i // 2, rows], low.at[i], load.at[i]))
        loads[-1].start()
    y_out[...] = y[...].reshape(y_out.shape)
    dx_out[...] = dx[...].reshape(dx_out.shape)
    for r in range(8):
        rest[r][...] = vec[r, :]
    for r in range(TILES):
        rest[8][r * D : (r + 1) * D] = vec[8 + r, :]
    stores = []
    for i, copy in enumerate(loads):
        block, part = divmod(i, 2)
        rows = slice(part * half, (part + 1) * half)
        if block < 4:
            target = down.at[slice(block * D + part * half, block * D + (part + 1) * half)]
        elif block < 8:
            target = up.at[rows, slice((block - 4) * D, (block - 3) * D)]
        else:
            target = (wq, wk, wv, wo)[block - 8].at[rows]
        copy.wait()
        high[i] = low[i].astype(f32)
        stores.append(pltpu.make_async_copy(high.at[i], target, store.at[i]))
        stores[-1].start()
    for copy in stores:
        copy.wait()


def widen(sums, vec, y, dx, shape):
    struct = jax.ShapeDtypeStruct
    square = struct((D, D), f32)
    vectors = [struct((D,), f32)] * 8 + [struct((FF,), f32)]
    chunks = 4 * OWN
    return pl.pallas_call(
        widen_kernel,
        out_shape=[struct((FF, D), f32), struct((D, FF), f32)]
        + [square] * 4
        + [struct(shape, bf16)] * 2
        + vectors,
        in_specs=[anywhere, in_vmem, in_vmem, in_vmem],
        out_specs=[anywhere] * 6 + [in_vmem] * 11,
        scratch_shapes=[
            pltpu.VMEM((chunks, D // 2, D), bf16),
            pltpu.VMEM((chunks, D // 2, D), f32),
            pltpu.SemaphoreType.DMA((chunks,)),
            pltpu.SemaphoreType.DMA((chunks,)),
        ],
        compiler_params=pltpu.CompilerParams(vmem_limit_bytes=VMEM_LIMIT),
    )(sums, vec, y, dx)


def body(
    tokens,
    cotangent,
    group_ids,
    random_blocks,
    norm1_gain,
    norm1_bias,
    query_weight,
    query_bias,
    key_weight,
    value_weight,
    value_bias,
    out_weight,
    out_bias,
    norm2_gain,
    norm2_bias,
    up_weight,
    up_bias,
    down_weight,
    down_bias,
):
    seqs, wins = lax.axis_size("seq"), lax.axis_size("win")
    windows, here, _ = tokens.shape
    length = here * seqs
    blocks = length // BLOCK
    rows = windows * here
    group = seqs // 2
    pairs = -(-HEADS // group)
    slots = pairs * group
    layer_steps = (seqs // 8).bit_length() - 1
    extra = -(-(HEAD_DIM + 3 * blocks) // 128) * 128 - HEAD_DIM
    dims = (wins, seqs, windows, pairs)
    struct = jax.ShapeDtypeStruct
    dma = pltpu.SemaphoreType.DMA
    vmem = pltpu.VMEM

    x = tokens.reshape(rows, D)
    layer_slots = max(layer_steps, 1)
    pieces = 2 * OWN
    early = TILES if length <= 2048 else 1
    y, dx, vec_sums, sums = pl.pallas_call(
        functools.partial(layer_kernel, dims),
        out_shape=(
            struct((rows, D), bf16),
            struct((rows, D), bf16),
            struct((VEC_ROWS, D), f32),
            struct((pieces, D, D), bf16),
        ),
        in_specs=[in_smem] + [in_vmem] * 10 + [anywhere] * 8,
        out_specs=(in_vmem, in_vmem, in_vmem, anywhere),
        scratch_shapes=[
            pltpu.SMEM((RAND, windows, blocks), jnp.int32),
            vmem((pieces, D, D), bf16),
            vmem((rows, D), bf16),
            vmem((2, here, D), bf16),
            vmem((2, here, D), bf16),
            vmem((3, D, D), bf16),
            vmem((D, D), bf16),
            vmem((rows, D), bf16),
            vmem((2, D, rows), bf16),
            vmem((4, rows, D), bf16),
            vmem((D, rows), bf16),
            vmem((TILES, D, rows), bf16),
            vmem((TILES, rows, D), bf16),
            vmem((rows, D), f32),
            vmem((early, rows, D) if early > 1 else (1, 8, 128), f32),
            vmem((8, D), f32),
            vmem((rows, D), bf16),
            vmem((D, rows), bf16),
            vmem((2, D, rows), bf16),
            vmem((2, rows, D), bf16),
            vmem((2, D, rows), bf16),
            vmem((4, rows, HALF), bf16),
            vmem((slots, 3 * HEAD_DIM, rows), bf16),
            vmem((group, pairs, 3 * HEAD_DIM, rows), bf16),
            vmem((slots, HEAD_DIM, rows), bf16),
            vmem((group, pairs, HEAD_DIM, rows), bf16),
            vmem((group, pairs, HEAD_DIM, rows), bf16),
            vmem((group, pairs, 3 * HEAD_DIM, rows), bf16),
            vmem((extra, length), bf16),
            vmem((pairs, HEAD_DIM, length), f32),
            vmem((pairs, 1, length), f32),
            vmem((length, HEAD_DIM + extra), bf16),
            vmem((HEAD_DIM, length), bf16),
            vmem((HEAD_DIM, length), bf16),
            vmem((wins, 8, 128), f32),
            vmem((pieces, D // 2, HALF), bf16),
            vmem((pieces, D // 4, HALF), bf16),
            vmem((pieces, D // 8, HALF), bf16),
            vmem((pieces, D // 16, HALF), bf16),
            vmem((pieces, layer_slots, D // 16, HALF), bf16),
            vmem((5, VEC_ROWS, D), f32),
            vmem((7 + layer_slots, VEC_ROWS, D), f32),
            dma((6 + 2 * TILES,)),
            dma,
            dma((pieces,)),
            dma((pieces, 9 + layer_steps)),
            pltpu.SemaphoreType.REGULAR((pieces,)),
            pltpu.SemaphoreType.REGULAR,
            dma((12,)),
            dma((12,)),
        ]
        + [dma((pairs, 2))] * 2
        + [dma((pairs, 1))] * 6
        + [dma((wins,))] * 2
        + [dma((6 + layer_steps,))] * 2
        + [dma((4,))] * 2,
        compiler_params=pltpu.CompilerParams(
            collective_id=0, has_side_effects=True, vmem_limit_bytes=VMEM_LIMIT
        ),
    )(
        group_ids, x, norm1_gain, norm1_bias, query_bias, value_bias, out_bias,
        norm2_gain, norm2_bias, up_bias, down_bias, jnp.transpose(random_blocks, (2, 0, 1)), cotangent.reshape(rows, D), query_weight,
        key_weight, value_weight, out_weight, up_weight, down_weight,
    )

    (
        down_grad, up_grad, query_grad, key_grad, value_grad, out_grad, output, input_grad,
        gain1_grad, shift1_grad, query_bias_grad, value_bias_grad, out_bias_grad,
        gain2_grad, shift2_grad, down_bias_grad, up_bias_grad,
    ) = widen(sums, vec_sums, y, dx, tokens.shape)
    return (
        output, input_grad, gain1_grad, shift1_grad, query_grad, query_bias_grad, key_grad,
        value_grad, value_bias_grad, out_grad, out_bias_grad, gain2_grad, shift2_grad, up_grad,
        up_bias_grad, down_grad, down_bias_grad,
    )


def solution(mesh):
    split = P("win", "seq", None)
    return jax.shard_map(
        body,
        mesh=mesh,
        in_specs=(split, split, P("win"), P("win", None, None)) + (P(),) * 15,
        out_specs=(split, split) + (P(),) * 15,
        check_vma=False,
    )
```

```python
import functools
import math

import jax
import jax.numpy as jnp
from jax import lax
from jax.experimental import pallas as pl
from jax.experimental.pallas import tpu as pltpu
from jax.sharding import PartitionSpec as P

D = 768
HEADS = 12
HEAD_DIM = 64
FF = 3072
BLOCK = 64
RAND = 3
GROUPS = 8
TILES = FF // D
VEC_ROWS = 16
OWN = 6
HALF = D // 2
VECTORS = 12
ORDERS = (
    "labh", "balh", "ablh", "balh",
    "ablh", "balh", "ablh", "balh",
    "ablh", "balh", "ablh", "balh",
)
SCHEDULE = (
    "2014AAA25403216057Wv36124v0X875v936b8v1a",
    "932v67405vb71a3v82109684a2b59713426a08b5",
    "97132641a526308b90754a8b594a36b8376a9b77",
    "8989abab",
)

MESH = pl.DeviceIdType.MESH
VMEM_LIMIT = 63 << 20
epsilon = 1e-05
masked_score = -1e30
score_scale = HEAD_DIM ** (-0.5)
f32 = jnp.float32
bf16 = jnp.bfloat16

in_vmem = pl.BlockSpec(memory_space=pltpu.VMEM)
in_smem = pl.BlockSpec(memory_space=pltpu.SMEM)
anywhere = pl.BlockSpec(memory_space=pl.ANY)


def mm(left, right):
    return jnp.dot(left, right, preferred_element_type=f32)


def mm_nt(left, right):
    return lax.dot_general(left, right, (((1,), (1,)), ((), ())), preferred_element_type=f32)


def row(ref):
    return ref[...].reshape(1, -1)


def normalise(v):
    centre = v - jnp.mean(v, axis=-1, keepdims=True)
    rstd = lax.rsqrt(jnp.mean(centre * centre, axis=-1, keepdims=True) + epsilon)
    return centre * rstd, rstd


def norm_back(err, vhat, rstd, gain):
    g = err * gain
    dv = rstd * (
        g - jnp.mean(g, axis=-1, keepdims=True) - vhat * jnp.mean(g * vhat, axis=-1, keepdims=True)
    )
    return dv, jnp.sum(err * vhat, axis=0, keepdims=True), jnp.sum(err, axis=0, keepdims=True)


def rcopy(src, dst, send, recv, device):
    return pltpu.make_async_remote_copy(
        src, dst, send, recv, device_id=device, device_id_type=MESH
    )


def span(start, size):
    return pl.ds(pl.multiple_of(start, 16), size)


class Place:
    def __init__(self, wins, seqs):
        self.wins, self.seqs = wins, seqs
        self.layers = seqs // 8
        self.w = lax.axis_index("win")
        self.s = lax.axis_index("seq")
        self.c = lax.rem(self.s, 2)
        self.z = lax.rem(self.s // 2, 4)
        self.layer = self.s // 8
        self.layer_steps = (seqs // 8).bit_length() - 1
        self.size = seqs // 2
        self.window = self.s // self.size
        self.g = lax.rem(self.s, self.size)
        self.base = self.s - self.g
        self.core_free = None
        self.bits = {"a": lax.rem(self.w, 2), "b": self.w // 2}

    def core(self):
        return (self.w, self.s + 1 - 2 * self.c)

    def across(self, axis):
        step = 1 if axis == "a" else 2
        return (self.w + step - 2 * step * self.bits[axis], self.s)

    def along(self, k):
        return (self.w, self.layer * 8 + lax.rem(self.z + k, 4) * 2 + self.c)

    def layer_swap(self, i):
        step = 2**i
        bit = lax.rem(self.layer // step, 2)
        return (self.w, self.s + 8 * step * (1 - 2 * bit))

    def step_z(self, step):
        bit = lax.rem(self.z // step, 2)
        return (self.w, self.s + 2 * step * (1 - 2 * bit))

    def core_open(self):
        if self.core_free is not None:
            pl.semaphore_wait(self.core_free, 1)
            self.core_free = None

    def group_at(self, k):
        return (self.w, self.base + lax.rem(self.g + k, self.size))

    def partner(self):
        return (self.w, lax.rem(self.s + self.size, self.seqs))

    def win_at(self, k):
        return (lax.rem(self.w + k, self.wins), self.s)

    def greet(self):
        barrier = pltpu.get_barrier_semaphore()

        def one(k, carry):
            pl.semaphore_signal(barrier, inc=1, device_id=self.group_at(k), device_id_type=MESH)
            return carry

        lax.fori_loop(1, self.size, one, 0)
        others = [self.partner()]
        others += [self.win_at(k) for k in range(1, self.wins)]
        others += [self.layer_swap(i) for i in range(self.layer_steps)]
        for peer in others:
            pl.semaphore_signal(barrier, inc=1, device_id=peer, device_id_type=MESH)
        pl.semaphore_wait(barrier, self.size - 1 + len(others))


class Exchange:
    def __init__(self, place, pairs, out, into, send, recv):
        self.place, self.pairs = place, pairs
        self.out, self.into, self.send, self.recv = out, into, send, recv

    def copy(self, k, pair, part, lanes):
        place = self.place
        target = lax.rem(place.g + k, place.size)
        return rcopy(
            self.out.at[target * self.pairs + pair, :, lanes],
            self.into.at[place.g, pair, :, lanes],
            self.send.at[pair, part],
            self.recv.at[pair, part],
            place.group_at(k),
        )

    def start(self, pair, part=0, lanes=slice(None)):
        def one(k, carry):
            self.copy(k, pair, part, lanes).start()
            return carry

        place = self.place
        lax.fori_loop(1, place.size, one, 0)
        self.into[place.g, pair, :, lanes] = self.out[place.g * self.pairs + pair, :, lanes]

    def whole(self, ref, pair, part, lanes):
        return rcopy(
            ref, ref, self.send.at[pair, part], self.recv.at[pair, part], self.place.group_at(1)
        )

    def arrived(self, pair, part=0, lanes=slice(None)):
        held = self.into.at[pl.ds(0, self.place.size - 1), pair, :, lanes]
        self.whole(held, pair, part, lanes).wait_recv()

    def sent(self, pair, part=0, lanes=slice(None)):
        held = self.out.at[pl.ds(0, self.place.size - 1), :, lanes]
        self.whole(held, pair, part, lanes).wait_send()


Q_ROWS, K_ROWS, V_ROWS = (slice(i * HEAD_DIM, (i + 1) * HEAD_DIM) for i in range(3))


def tile_width(length):
    return 256 if length <= 2048 else 128


def block_at(place, first, shape, axis):
    index = first + lax.broadcasted_iota(jnp.int32, shape, axis)
    slot, half = index // 256, lax.rem(index // 128, 2)
    window = place.window + half - 2 * half * place.window
    return (window * place.size + slot) * 2 + lax.rem(index // BLOCK, 2)


def block_ones(place, keys, blocks):
    length, lanes = keys.shape

    def one_group(group, carry):
        shape = (256, lanes)
        part = lax.broadcasted_iota(jnp.int32, shape, 1) - HEAD_DIM
        block = block_at(place, group * 256, shape, 0)
        hit = (part == block) | (part == block + blocks) | (part == block + 2 * blocks)
        keys[span(group * 256, 256), :] = jnp.where(hit, 1.0, 0.0).astype(bf16)
        return carry

    lax.fori_loop(0, length // 256, one_group, 0)


def gather_rows(ref, pair, rows, into):
    tokens = ref.shape[3]
    for s in range(ref.shape[0]):
        into[: rows.stop - rows.start, s * tokens : (s + 1) * tokens] = ref[s, pair, rows, :]


def place_of_tile(tile, width):
    per_slot = 256 // width
    if per_slot == 1:
        return tile, slice(None)
    return tile // per_slot, pl.ds(pl.multiple_of(lax.rem(tile, per_slot) * width, width), width)


def biased_scores(keys, q_t, bias, lanes):
    return mm(keys[...], jnp.concatenate([q_t, bias[:, lanes]], axis=0))


def attend_pair(pair, qkv, bias, keys, k_t, v_t, small_out, raw, mass):
    length = v_t.shape[1]
    pairs = qkv.shape[1]
    width = tile_width(length)
    step = length if length <= 1024 else 512
    gather_rows(qkv, pair, K_ROWS, k_t)
    gather_rows(qkv, pair, V_ROWS, v_t)
    keys[:, :HEAD_DIM] = k_t[...].T

    def one_tile(tile, carry):
        lanes = pl.ds(pl.multiple_of(tile * width, width), width)
        slot, within = place_of_tile(tile, width)
        q_t = qkv[slot, pair, Q_ROWS, within]
        parts = [slice(first, first + step) for first in range(0, length, step)]
        scores = [biased_scores(keys.at[part], q_t, bias, lanes) for part in parts]
        top = jnp.max(scores[0], axis=0, keepdims=True)
        for more in scores[1:]:
            top = jnp.maximum(top, jnp.max(more, axis=0, keepdims=True))
        total, got = 0.0, 0.0
        for i, part in enumerate(parts):
            held = scores[0] if len(parts) == 1 else biased_scores(keys.at[part], q_t, bias, lanes)
            weight = jnp.exp(held - top)
            total = total + jnp.sum(weight, axis=0, keepdims=True)
            got = got + mm(v_t[:, part], weight.astype(bf16))
        mass[pair, :, lanes] = top + jnp.log(total)
        got = got * (1.0 / total)
        raw[pair, :, lanes] = got
        small_out[slot * pairs + pair, :, within] = got.astype(bf16)
        return carry

    lax.fori_loop(0, length // width, one_tile, 0)


def attend_pair_back(pair, qkv, grad, bias, raw, mass, keys, k_t, v_t, dk, dv, out):
    length = v_t.shape[1]
    pairs = qkv.shape[1]
    width = tile_width(length)
    step = length if length <= 1024 else 512
    gather_rows(qkv, pair, K_ROWS, k_t)
    gather_rows(qkv, pair, V_ROWS, v_t)
    keys[:, :HEAD_DIM] = k_t[...].T
    values = v_t[...].T
    dk[...] = jnp.zeros_like(dk)
    dv[...] = jnp.zeros_like(dv)

    def one_tile(tile, carry):
        lanes = pl.ds(pl.multiple_of(tile * width, width), width)
        slot, within = place_of_tile(tile, width)
        q_t = qkv[slot, pair, Q_ROWS, within]
        g_t = grad[slot, pair, :, within]
        row_dot = jnp.sum(g_t.astype(f32) * raw[pair, :, lanes], axis=0, keepdims=True)
        dq = jnp.zeros(q_t.shape, f32)
        for first in range(0, length, step):
            part = slice(first, first + step)
            probs = jnp.exp(biased_scores(keys.at[part], q_t, bias, lanes) - mass[pair, :, lanes])
            score_grad = (probs * (mm(values[part], g_t) - row_dot)).astype(bf16)
            dq = dq + mm(k_t[:, part], score_grad)
            dk[:, part] += mm_nt(q_t, score_grad)
            dv[:, part] += mm_nt(g_t, probs.astype(bf16))
        out[slot * pairs + pair, Q_ROWS, within] = (dq * score_scale).astype(bf16)
        return carry

    lax.fori_loop(0, length // width, one_tile, 0)
    dk_t, dv_t = dk[...].astype(bf16), dv[...].astype(bf16)
    for slot in range(qkv.shape[0]):
        lanes = slice(slot * 256, (slot + 1) * 256)
        out[slot * pairs + pair, K_ROWS, :] = dk_t[:, lanes]
        out[slot * pairs + pair, V_ROWS, :] = dv_t[:, lanes]


def project_qkv(half, xs, gain, shift, weights, biases, out, n1_t, wait):
    tokens = xs.shape[0] // 2
    here = slice(half * tokens, (half + 1) * tokens)
    vhat, _ = normalise(xs[here, :].astype(f32))
    n1 = (vhat * row(gain) + row(shift)).astype(bf16)
    n1_t[:, here] = n1.T
    for part in range(3):
        wait(part)
        y = mm(n1, weights[part])
        if biases[part] is not None:
            y = y + row(biases[part])
        y = y.astype(bf16)
        if part == 0:
            y = y * jnp.asarray(score_scale, bf16)
        y_t = y.T
        for h in range(HEADS):
            out[h, part * HEAD_DIM : (part + 1) * HEAD_DIM, here] = y_t[
                h * HEAD_DIM : (h + 1) * HEAD_DIM, :
            ]


def fill_bias(place, picks, bias, blocks):
    rows, length = bias.shape
    bias[...] = jnp.zeros_like(bias)

    def one_group(group, carry):
        lanes = pl.ds(pl.multiple_of(group * 128, 128), 128)
        key = lax.broadcasted_iota(jnp.int32, (blocks, 128), 0)
        query = block_at(place, group * 128, (blocks, 128), 1)
        count = (
            jnp.where((key == query - 1) & (query > 0), 1.0, 0.0)
            + jnp.where(key == query, 1.0, 0.0)
            + jnp.where((key == query + 1) & (query < blocks - 1), 1.0, 0.0)
            + jnp.where(key == 0, 1.0, 0.0)
            + jnp.where(key == blocks - 1, 1.0, 0.0)
        )
        half = lax.rem(group, 2)
        window = place.window + half - 2 * half * place.window
        first = (window * place.size + group // 2) * 2
        for side in range(2):
            for r in range(RAND):
                pick = picks[r, place.window, first + side]
                count = count + jnp.where((key == pick) & (query == first + side), 1.0, 0.0)
        listed = count > 0.0
        rest = jnp.where(listed, jnp.log(jnp.maximum(count, 1.0)), masked_score)
        for term in range(3):
            part = rest.astype(bf16)
            bias[term * blocks : (term + 1) * blocks, lanes] = part
            rest = jnp.where(listed, rest - part.astype(f32), 0.0)
        return carry

    lax.fori_loop(0, length // 128, one_group, 0)


def input_back(xs, gain, grad_in, hg, weights, rhs, vec):
    pairs = grad_in.shape[1]
    vhat, rstd = normalise(xs[...].astype(f32))
    err = jnp.zeros(vhat.shape, f32)
    slots = [divmod(h, pairs) for h in range(HEADS)]
    for part in range(3):
        rows = slice(part * HEAD_DIM, (part + 1) * HEAD_DIM)
        rhs[part] = jnp.concatenate([grad_in[s, p, rows, :] for s, p in slots], axis=0).T
        grad = rhs[part]
        err = err + mm_nt(grad, weights[part])
        if part != 1:
            r = 2 + part // 2
            vec[r : r + 1, :] = jnp.sum(grad.astype(f32), axis=0, keepdims=True)
    dv, dgain, dshift = norm_back(err, vhat, rstd, row(gain))
    vec[0:1, :] = dgain
    vec[1:2, :] = dshift
    return (hg[...] + dv).astype(bf16)


def reduce_piece(place, order, out, out_hbm, store, mine, other, bufs, rl, send, recv, free):
    index, col = mine
    cols = pl.ds(col, HALF)
    buf = out.at[index]
    ways = {
        "a": (place.bits["a"], place.across("a")),
        "b": (place.bits["b"], place.across("b")),
        "l": (lax.rem(place.z, 2), place.step_z(1)),
        "h": (place.z // 2, place.step_z(2)),
    }
    hops = [ways[axis] for axis in order]

    def at(start, size):
        return buf.at[span(start, size), cols]

    start, size = 0, D
    spans = []
    for i, (bit, partner) in enumerate(hops):
        size = size // 2
        keep, away = start + bit * size, start + (1 - bit) * size
        if i:
            source = bufs[i - 1]
            at(away, size)[...] = at(away, size)[...] + source[span((1 - bit) * size, size)]
        cp = rcopy(at(away, size), bufs[i], send, recv.at[i], partner)
        cp.start()
        if i:
            at(keep, size)[...] = at(keep, size)[...] + source[span(bit * size, size)]
        start = keep
        spans.append((keep, size))
        yield
        cp.wait()
        pl.semaphore_signal(free, inc=1, device_id=partner, device_id_type=MESH)
    held = at(start, size)
    held[...] = held[...] + bufs[-1][...]
    for i in range(place.layer_steps):
        cp = rcopy(held, rl.at[i], send, recv.at[9 + i], place.layer_swap(i))
        cp.start()
        cp.wait()
        held[...] = held[...] + rl[i]
    pl.semaphore_wait(free, len(hops))
    for i in reversed(range(len(hops))):
        held = at(*spans[i])
        cp = rcopy(held, held, send, recv.at[4 + i], hops[i][1])
        cp.start()
        yield
        cp.wait()
    place.core_open()
    held = buf.at[:, cols]
    cp = rcopy(held, held, send, recv.at[8], place.core())
    cp.start()
    yield
    cp.wait()
    for block, column in (mine, other):
        where = (block, slice(None), pl.ds(column, HALF))
        pltpu.make_async_copy(out.at[where], out_hbm.at[where], store).start()


def reduce_vectors(place, out, run, got, send, recv):
    for step, device in enumerate((place.core(), place.across("a"), place.across("b"))):
        cp = rcopy(run.at[step], got.at[step], send.at[step], recv.at[step], device)
        cp.start()
        yield
        cp.wait()
        run[step + 1] = run[step] + got[step]
    got[3 + place.z] = run[3]
    cps = [
        rcopy(run.at[3], got.at[3 + place.z], send.at[2 + k], recv.at[6 - k], place.along(k))
        for k in (1, 2, 3)
    ]
    for cp in cps:
        cp.start()
    yield
    for cp in cps:
        cp.wait_send()
    for k in (1, 2, 3):
        slot = got.at[3 + lax.rem(place.z + k, 4)]
        rcopy(slot, slot, send.at[2 + k], recv.at[2 + k], place.along(k)).wait_recv()
    total = got[3]
    for k in range(1, 4):
        total = total + got[3 + k]
    for i in range(place.layer_steps):
        run[4] = total
        cp = rcopy(run.at[4], got.at[7 + i], send.at[6 + i], recv.at[6 + i], place.layer_swap(i))
        cp.start()
        cp.wait()
        total = total + got[7 + i]
    out[...] = total


def layer_kernel(
    dims,
    ids, x, gain1, shift1, bq, bv, bo, gain2, shift2, bup, bdown,
    picks_hbm, cot_hbm, wq_hbm, wk_hbm, wv_hbm, wo_hbm, wup_hbm, wdown_hbm,
    y, dx, vec_out, out_hbm,
    picks, out, xs, y_sent, y_got, wqkv, wo, og, lhs, rhs, n2_t, act_t, pg, hg, dact, up_bias,
    s_og, s_n2, s_act, s_pg, s_lhs, s_rhs,
    head_out, by_head, small_out, att_in, do_in, dqkv_in, bias, raw, mass, keys, k_t, v_t, counts,
    r0, r1, r2, r3, rl, run, got,
    load, store, piece_send, piece_recv, free, core_free, core_send, core_recv,
    qkv_send, qkv_recv, att_send, att_recv, do_send, do_recv, dqkv_send, dqkv_recv,
    count_send, count_recv, vec_send, vec_recv, swap_send, swap_recv,
):
    wins, seqs, windows, pairs = dims
    place = Place(wins, seqs)
    c = place.c
    tokens = x.shape[0] // windows
    kept = pl.ds(pl.multiple_of(place.window * tokens, tokens), tokens)
    moved = pl.ds(pl.multiple_of((1 - place.window) * tokens, tokens), tokens)
    lower, upper = slice(0, tokens), slice(tokens, 2 * tokens)
    length = v_t.shape[1]
    blocks = length // BLOCK
    theirs, ours = 2 * (1 - c), 2 * c

    def up_tile(t):
        return out.at[(t // 2) * 4 + theirs + lax.rem(t, 2)]

    def down_tile(t):
        return out.at[8 + t]

    moves = [(wq_hbm, wqkv.at[0]), (wk_hbm, wqkv.at[1]), (wv_hbm, wqkv.at[2])]
    moves += [(cot_hbm.at[kept], og.at[lower])]
    moves += [(wdown_hbm.at[t * D : (t + 1) * D], down_tile(t)) for t in range(TILES)]
    moves += [(wo_hbm, wo), (picks_hbm, picks)]
    moves += [(wup_hbm.at[:, t * D : (t + 1) * D], up_tile(t)) for t in range(TILES)]
    loads = [pltpu.make_async_copy(src, dst, load.at[i]) for i, (src, dst) in enumerate(moves)]
    for copy in loads:
        copy.start()
    place.greet()

    def swap(i, src, dst):
        copy = rcopy(src, dst, swap_send.at[i], swap_recv.at[i], place.partner())
        copy.start()
        return copy

    x_swap = swap(0, x.at[moved], xs.at[upper])
    lane = lax.broadcasted_iota(jnp.int32, (8, 128), 1)
    member = [jnp.where(lane == ids[w], 1.0, 0.0) for w in range(windows)]
    counts[place.w] = sum(member[1:], member[0])
    mine = counts.at[place.w]
    count_moves = [
        rcopy(mine, mine, count_send.at[k], count_recv.at[k], place.win_at(k))
        for k in range(1, wins)
    ]
    for copy in count_moves:
        copy.start()
    for t in range(TILES):
        up_bias[t : t + 1, :] = bup[t * D : (t + 1) * D].reshape(1, D)
    for p in range(HEADS, head_out.shape[0]):
        head_out[p] = jnp.zeros(head_out.shape[1:], bf16)

    qkv_moves = Exchange(place, pairs, head_out, by_head, qkv_send, qkv_recv)
    att_moves = Exchange(place, pairs, small_out, att_in, att_send, att_recv)
    do_moves = Exchange(place, pairs, small_out, do_in, do_send, do_recv)
    dqkv_moves = Exchange(place, pairs, head_out, dqkv_in, dqkv_send, dqkv_recv)
    halves = (lower, upper)
    xs[lower, :] = x[kept, :]
    for half in range(2):
        if half:
            block_ones(place, keys, blocks)
            loads[5 + TILES].wait()
            fill_bias(place, picks, bias, blocks)
            x_swap.wait()
            cot_swap = swap(1, cot_hbm.at[moved], og.at[upper])
        project_qkv(
            half, xs, gain1, shift1, wqkv, (bq, None, bv), head_out, lhs.at[0],
            (lambda part: None) if half else (lambda part: loads[part].wait()),
        )
        for pair in range(pairs):
            qkv_moves.start(pair, half, halves[half])

    core_moves = {}

    def to_core(name, src, dst):
        i = len(core_moves)
        core_moves[name] = rcopy(src, dst, core_send.at[i], core_recv.at[i], place.core())
        core_moves[name].start()

    waited = set()

    def from_core(*names):
        for name in names:
            if name not in waited:
                waited.add(name)
                core_moves[name].wait()

    to_core("n1", lhs.at[0], s_lhs.at[0])

    for pair in range(pairs):
        for half in range(2):
            qkv_moves.arrived(pair, half, halves[half])
        attend_pair(pair, by_head, bias, keys, k_t, v_t, small_out, raw, mass)
        att_moves.start(pair)
    for copy in count_moves:
        copy.wait_send()
    for k in range(1, wins):
        slot = counts.at[lax.rem(place.w + wins - k, wins)]
        rcopy(slot, slot, count_send.at[k], count_recv.at[k], place.win_at(k)).wait_recv()
    sizes = counts[0]
    for k in range(1, wins):
        sizes = sizes + counts[k]
    first_row = lax.broadcasted_iota(jnp.int32, (8, 128), 0) == 0
    loads[3].wait()
    cot_swap.wait()
    own_size = jnp.sum(
        jnp.where(first_row & (lane == ids[place.window]), sizes, 0.0), keepdims=True
    )
    og[...] = (og[...].astype(f32) * (windows * wins / (GROUPS * own_size))).astype(bf16)
    to_core("og", og, s_og)
    out_grad = og[...]
    for t in range(TILES):
        loads[4 + t].wait()
    early = dact.shape[0] > 1
    if early:
        for t in range(TILES):
            dact[t] = mm_nt(out_grad, down_tile(t)[...])

    for pair in range(pairs):
        att_moves.arrived(pair)
    for h in range(HEADS):
        slot, pair = divmod(h, pairs)
        lhs[1, h * HEAD_DIM : (h + 1) * HEAD_DIM, :] = att_in[slot, pair]
    to_core("att", lhs.at[1], s_lhs.at[1])
    for copy in [loads[4 + TILES]] + loads[6 + TILES :]:
        copy.wait()


    def fill(index, cols, parts):
        @pl.loop(0, D // 256)
        def _(i):
            rows = span(i * 256, 256)
            (left, right), (left2, right2) = parts
            total = mm(left[rows, :], right) + mm(left2[rows, :], right2)
            out[index, rows, cols] = total.astype(bf16)

    def stream(p):
        if p < 8:
            i, h = (p % 4) // 2, p % 2
            index, other = (p // 4) * 4 + ours + i, (p // 4) * 4 + theirs + i
            col = other_col = h * HALF
            cols = slice(col, col + HALF)
            if p < 4:
                from_core("og", ("act", i))
                parts = ((act_t.at[ours + i], og[:, cols]), (s_act.at[i], s_og[:, cols]))
            else:
                from_core("n2", ("pg", i))
                parts = ((n2_t, pg[ours + i, :, cols]), (s_n2, s_pg[i, :, cols]))
        else:
            i = (3, 0, 1, 2)[p - 8]
            index = other = 8 + i
            col = pl.multiple_of(c * HALF, HALF)
            other_col = pl.multiple_of((1 - c) * HALF, HALF)
            cols = pl.ds(col, HALF)
            side = i // 3
            from_core(("n1", "att")[side], ("rhs", i))
            parts = ((lhs.at[side], rhs[i, :, cols]), (s_lhs.at[side], s_rhs[i]))
        fill(index, cols, parts)
        return reduce_piece(
            place, ORDERS[p], out, out_hbm, store,
            (index, col), (other, other_col),
            [ref.at[p] for ref in (r0, r1, r2, r3)],
            *(ref.at[p] for ref in (rl, piece_send, piece_recv, free)),
        )

    streams = {}
    ended = set()

    def go(p):
        if p not in streams:
            if p == VECTORS:
                streams[p] = reduce_vectors(place, vec_out, run, got, vec_send, vec_recv)
            else:
                streams[p] = stream(p)
        if p not in ended and next(streams[p], True) is not None:
            ended.add(p)


    hidden = xs[...].astype(f32) + (mm(lhs[1].T, wo[...]) + row(bo))
    vhat, rstd = normalise(hidden)
    n2 = (vhat * row(gain2) + row(shift2)).astype(bf16)
    n2_t[...] = n2.T
    to_core("n2", n2_t, s_n2)
    vec = run.at[0]
    vec[...] = jnp.zeros_like(vec)
    total = jnp.zeros(hidden.shape, f32)
    err = jnp.zeros(hidden.shape, f32)
    for i in range(TILES):
        t = (theirs if i < 2 else ours) + i % 2
        up_part, down_part = up_tile(t)[...], down_tile(t)[...]
        pre = mm(n2, up_part) + up_bias[pl.ds(t, 1), :]
        phi = 0.5 * (1.0 + lax.erf(pre * (0.5**0.5)))
        act = (pre * phi).astype(bf16)
        act_t[t] = act.T
        slope = phi + pre * (jnp.exp(-0.5 * pre * pre) * (1.0 / math.sqrt(2.0 * math.pi)))
        back = dact[t] if early else mm_nt(out_grad, down_part)
        grad = (back * slope).astype(bf16)
        pg[t] = grad
        if i < 2:
            to_core(("act", i), act_t.at[t], s_act.at[i])
            to_core(("pg", i), pg.at[t], s_pg.at[i])
        total = total + mm(act, down_part)
        err = err + mm_nt(grad, up_part)
        vec[pl.ds(8 + t, 1), :] = jnp.sum(grad.astype(f32), axis=0, keepdims=True)
        if i == 2:
            for p in (0, 1, 4, 5):
                go(p)
    pl.semaphore_signal(core_free, inc=1, device_id=place.core(), device_id_type=MESH)
    place.core_free = core_free
    dv, dgain, dshift = norm_back(err, vhat, rstd, row(gain2))
    hidden_grad = out_grad.astype(f32) + dv
    branch = hidden_grad.astype(bf16)
    rhs[3] = branch
    datt_t = mm_nt(branch, wo[...]).astype(bf16).T
    for pair in range(pairs):
        att_moves.sent(pair)
    small_out[:HEADS] = datt_t.reshape(HEADS, HEAD_DIM, 2 * tokens)
    for pair in range(pairs):
        do_moves.start(pair)
    their_cols = pl.ds(pl.multiple_of((1 - c) * HALF, HALF), HALF)
    to_core(("rhs", 3), rhs.at[3, :, their_cols], s_rhs.at[3])
    hg[...] = hidden_grad
    result = (hidden + total + row(bdown)).astype(bf16)
    y[kept, :] = result[:tokens]
    y_sent[0] = result[tokens:]
    y_swap = swap(2, y_sent.at[0], y_got.at[0])
    vec[4:5, :] = jnp.sum(branch.astype(f32), axis=0, keepdims=True)
    vec[5:6, :] = dgain
    vec[6:7, :] = dshift
    vec[7:8, :] = jnp.sum(out_grad.astype(f32), axis=0, keepdims=True)
    for pair in range(pairs):
        for half in range(2):
            qkv_moves.sent(pair, half, halves[half])


    done_pairs = [0]

    def attention():
        pair = done_pairs[0]
        if pair == pairs:
            return
        done_pairs[0] += 1
        do_moves.arrived(pair)

        def scoped(dk, dv):
            attend_pair_back(
                pair, by_head, do_in, bias, raw, mass, keys, k_t, v_t, dk, dv, head_out
            )

        summed = pltpu.VMEM((HEAD_DIM, length), f32)
        pl.run_scoped(scoped, summed, summed)
        dqkv_moves.start(pair)

    def inputs():
        while done_pairs[0] < pairs:
            attention()
        for pair in range(pairs):
            dqkv_moves.arrived(pair)
        result = input_back(xs, gain1, dqkv_in, hg, wqkv, rhs, vec)
        for i in range(3):
            to_core(("rhs", i), rhs.at[i, :, their_cols], s_rhs.at[i])
        dx[kept, :] = result[:tokens]
        y_sent[1] = result[tokens:]
        swaps.append(swap(3, y_sent.at[1], y_got.at[1]))

    swaps = [y_swap]
    actions = {
        "A": attention,
        "W": inputs,
        "X": lambda: from_core(("rhs", 0), ("rhs", 1), ("rhs", 2)),
        "v": functools.partial(go, VECTORS),
    }
    for token in "".join(SCHEDULE):
        if token in actions:
            actions[token]()
        else:
            go(int(token, 16))
    everything = list(range(2 * OWN)) + [VECTORS]
    while len(ended) < len(everything):
        for p in everything:
            go(p)
    pltpu.make_async_copy(out, out_hbm, store).wait()
    from_core(*core_moves)
    for copy in swaps:
        copy.wait()
    y[moved, :] = y_got[0]
    dx[moved, :] = y_got[1]
    for pair in range(pairs):
        do_moves.sent(pair)
        dqkv_moves.sent(pair)


def widen_kernel(
    sums, vec, y, dx, down, up, wq, wk, wv, wo, y_out, dx_out, *rest
):
    low, high, load, store = rest[-4:]
    half = D // 2
    loads = []
    for i in range(4 * OWN):
        rows = slice((i % 2) * half, (i % 2 + 1) * half)
        loads.append(pltpu.make_async_copy(sums.at[i // 2, rows], low.at[i], load.at[i]))
        loads[-1].start()
    y_out[...] = y[...].reshape(y_out.shape)
    dx_out[...] = dx[...].reshape(dx_out.shape)
    for r in range(8):
        rest[r][...] = vec[r, :]
    for r in range(TILES):
        rest[8][r * D : (r + 1) * D] = vec[8 + r, :]
    stores = []
    for i, copy in enumerate(loads):
        block, part = divmod(i, 2)
        rows = slice(part * half, (part + 1) * half)
        if block < 4:
            target = down.at[slice(block * D + part * half, block * D + (part + 1) * half)]
        elif block < 8:
            target = up.at[rows, slice((block - 4) * D, (block - 3) * D)]
        else:
            target = (wq, wk, wv, wo)[block - 8].at[rows]
        copy.wait()
        high[i] = low[i].astype(f32)
        stores.append(pltpu.make_async_copy(high.at[i], target, store.at[i]))
        stores[-1].start()
    for copy in stores:
        copy.wait()


def widen(sums, vec, y, dx, shape):
    struct = jax.ShapeDtypeStruct
    square = struct((D, D), f32)
    vectors = [struct((D,), f32)] * 8 + [struct((FF,), f32)]
    chunks = 4 * OWN
    return pl.pallas_call(
        widen_kernel,
        out_shape=[struct((FF, D), f32), struct((D, FF), f32)]
        + [square] * 4
        + [struct(shape, bf16)] * 2
        + vectors,
        in_specs=[anywhere, in_vmem, in_vmem, in_vmem],
        out_specs=[anywhere] * 6 + [in_vmem] * 11,
        scratch_shapes=[
            pltpu.VMEM((chunks, D // 2, D), bf16),
            pltpu.VMEM((chunks, D // 2, D), f32),
            pltpu.SemaphoreType.DMA((chunks,)),
            pltpu.SemaphoreType.DMA((chunks,)),
        ],
        compiler_params=pltpu.CompilerParams(vmem_limit_bytes=VMEM_LIMIT),
    )(sums, vec, y, dx)


def body(
    tokens,
    cotangent,
    group_ids,
    random_blocks,
    norm1_gain,
    norm1_bias,
    query_weight,
    query_bias,
    key_weight,
    value_weight,
    value_bias,
    out_weight,
    out_bias,
    norm2_gain,
    norm2_bias,
    up_weight,
    up_bias,
    down_weight,
    down_bias,
):
    seqs, wins = lax.axis_size("seq"), lax.axis_size("win")
    windows, here, _ = tokens.shape
    length = here * seqs
    blocks = length // BLOCK
    rows = windows * here
    group = seqs // 2
    pairs = -(-HEADS // group)
    slots = pairs * group
    layer_steps = (seqs // 8).bit_length() - 1
    extra = -(-(HEAD_DIM + 3 * blocks) // 128) * 128 - HEAD_DIM
    dims = (wins, seqs, windows, pairs)
    struct = jax.ShapeDtypeStruct
    dma = pltpu.SemaphoreType.DMA
    vmem = pltpu.VMEM

    x = tokens.reshape(rows, D)
    layer_slots = max(layer_steps, 1)
    pieces = 2 * OWN
    early = TILES if length <= 2048 else 1
    y, dx, vec_sums, sums = pl.pallas_call(
        functools.partial(layer_kernel, dims),
        out_shape=(
            struct((rows, D), bf16),
            struct((rows, D), bf16),
            struct((VEC_ROWS, D), f32),
            struct((pieces, D, D), bf16),
        ),
        in_specs=[in_smem] + [in_vmem] * 10 + [anywhere] * 8,
        out_specs=(in_vmem, in_vmem, in_vmem, anywhere),
        scratch_shapes=[
            pltpu.SMEM((RAND, windows, blocks), jnp.int32),
            vmem((pieces, D, D), bf16),
            vmem((rows, D), bf16),
            vmem((2, here, D), bf16),
            vmem((2, here, D), bf16),
            vmem((3, D, D), bf16),
            vmem((D, D), bf16),
            vmem((rows, D), bf16),
            vmem((2, D, rows), bf16),
            vmem((4, rows, D), bf16),
            vmem((D, rows), bf16),
            vmem((TILES, D, rows), bf16),
            vmem((TILES, rows, D), bf16),
            vmem((rows, D), f32),
            vmem((early, rows, D) if early > 1 else (1, 8, 128), f32),
            vmem((8, D), f32),
            vmem((rows, D), bf16),
            vmem((D, rows), bf16),
            vmem((2, D, rows), bf16),
            vmem((2, rows, D), bf16),
            vmem((2, D, rows), bf16),
            vmem((4, rows, HALF), bf16),
            vmem((slots, 3 * HEAD_DIM, rows), bf16),
            vmem((group, pairs, 3 * HEAD_DIM, rows), bf16),
            vmem((slots, HEAD_DIM, rows), bf16),
            vmem((group, pairs, HEAD_DIM, rows), bf16),
            vmem((group, pairs, HEAD_DIM, rows), bf16),
            vmem((group, pairs, 3 * HEAD_DIM, rows), bf16),
            vmem((extra, length), bf16),
            vmem((pairs, HEAD_DIM, length), f32),
            vmem((pairs, 1, length), f32),
            vmem((length, HEAD_DIM + extra), bf16),
            vmem((HEAD_DIM, length), bf16),
            vmem((HEAD_DIM, length), bf16),
            vmem((wins, 8, 128), f32),
            vmem((pieces, D // 2, HALF), bf16),
            vmem((pieces, D // 4, HALF), bf16),
            vmem((pieces, D // 8, HALF), bf16),
            vmem((pieces, D // 16, HALF), bf16),
            vmem((pieces, layer_slots, D // 16, HALF), bf16),
            vmem((5, VEC_ROWS, D), f32),
            vmem((7 + layer_slots, VEC_ROWS, D), f32),
            dma((6 + 2 * TILES,)),
            dma,
            dma((pieces,)),
            dma((pieces, 9 + layer_steps)),
            pltpu.SemaphoreType.REGULAR((pieces,)),
            pltpu.SemaphoreType.REGULAR,
            dma((12,)),
            dma((12,)),
        ]
        + [dma((pairs, 2))] * 2
        + [dma((pairs, 1))] * 6
        + [dma((wins,))] * 2
        + [dma((6 + layer_steps,))] * 2
        + [dma((4,))] * 2,
        compiler_params=pltpu.CompilerParams(
            collective_id=0, has_side_effects=True, vmem_limit_bytes=VMEM_LIMIT
        ),
    )(
        group_ids, x, norm1_gain, norm1_bias, query_bias, value_bias, out_bias,
        norm2_gain, norm2_bias, up_bias, down_bias, jnp.transpose(random_blocks, (2, 0, 1)), cotangent.reshape(rows, D), query_weight,
        key_weight, value_weight, out_weight, up_weight, down_weight,
    )

    (
        down_grad, up_grad, query_grad, key_grad, value_grad, out_grad, output, input_grad,
        gain1_grad, shift1_grad, query_bias_grad, value_bias_grad, out_bias_grad,
        gain2_grad, shift2_grad, down_bias_grad, up_bias_grad,
    ) = widen(sums, vec_sums, y, dx, tokens.shape)
    return (
        output, input_grad, gain1_grad, shift1_grad, query_grad, query_bias_grad, key_grad,
        value_grad, value_bias_grad, out_grad, out_bias_grad, gain2_grad, shift2_grad, up_grad,
        up_bias_grad, down_grad, down_bias_grad,
    )


def solution(mesh):
    split = P("win", "seq", None)
    return jax.shard_map(
        body,
        mesh=mesh,
        in_specs=(split, split, P("win"), P("win", None, None)) + (P(),) * 15,
        out_specs=(split, split) + (P(),) * 15,
        check_vma=False,
    )
```
